32 devices in a mesh: groups: 2 (over y), tm: 4 (over z), rows: 4 (over x, core).
Axes of the slice: x: 2, y: 2, z: 4, core: 2. Of those that a mesh axis runs over, the one named last changes fastest.
Arguments:
- latents: bfloat16 [16, 16, 128, 256], P(('groups', 'tm'), 'rows'), parts along dimension 0, may hold values from -6 to 6
- weight_in: bfloat16 [3, 3, 256, 256], replicated, may hold values from -0.125 to 0.125
- weight_out: bfloat16 [3, 3, 256, 256], replicated, may hold values from -0.0234375 to 0.0234375
- decay_table: float32 [16], replicated, may hold values from 0.99 to 0.999
- decay_index: int32 [256], replicated, may hold values from 0 to 15
Outputs:
- updated: bfloat16 [16, 16, 128, 256], P(('groups', 'tm'), 'rows'), parts along dimension 0
The draws below stay inside these ranges and needn't reach their ends.
There are 2 independent parts, one for each index of `groups`. The reference program is written for one: setup_inputs(seed, part) draws one part's arguments, and reference() takes and returns one part's arrays. A program takes and returns all parts, laid end to end along the dimension named above; an argument that names none is the same for every part. Nothing has to cross between parts.
All inputs are finite; a program needn't handle non-finite values.
Results may differ from the reference program's by a relative error of at most 0.0032.
Values may be sent and summed in bfloat16 or wider, within the bound.
A program may use at most 64 MiB of HBM per device.

```python
import jax
import jax.numpy as jnp
from jax import lax

C = 256
W = 128
LEVELS = 16
FRAMES = 8
H = 16


def place_ends(drawn, stream_key, smallest, largest):
    longest = drawn.shape.index(max(drawn.shape))
    spots = []
    for shift in (0, 1):
        where = [jax.random.randint(jax.random.fold_in(stream_key, axis), (), 0, length) for axis, length in enumerate(drawn.shape)]
        where[longest] = (where[longest] + shift) % drawn.shape[longest]
        spots.append(tuple(where))
    return drawn.at[spots[0]].set(smallest).at[spots[1]].set(largest)


def block_levels(key, extent, pieces, low, largest):
    gain = 1.0
    for position, shards_of in pieces:
        draws = jax.random.uniform(jax.random.fold_in(jax.random.fold_in(key, 6), position), (shards_of,), jnp.float32, low / len(pieces), largest / len(pieces))
        gain = gain * jnp.repeat(jnp.exp(draws), extent[position] // shards_of).reshape((-1,) + (1,) * (len(extent) - 1 - position))
    return gain


def centred(stream_key, shape, scale, most, shards=(), dtype=jnp.bfloat16):
    gain = block_levels(stream_key, shape, shards, -0.22, 0.18) if shards else 1.0
    drawn = jax.random.normal(stream_key, shape, jnp.float32) * scale * gain
    return jnp.minimum(jnp.maximum(drawn, -most), most).astype(dtype)


def setup_inputs(seed: int = 0, part: int = 0) -> dict:
    key_list = jax.random.split(jax.random.key(seed), 6)
    part_keys = jax.random.split(jax.random.fold_in(key_list[5], part), 6)
    return {
        "latents": centred(part_keys[0], (FRAMES, H, W, C), 1.0, 6.0, ((0, 4), (1, 4))),
        "weight_in": centred(key_list[1], (3, 3, C, C), (9 * C) ** -0.5, 0.125),
        "weight_out": centred(key_list[2], (3, 3, C, C), (9 * C * 32) ** -0.5, 0.0234375),
        "decay_table": jnp.clip(jax.random.uniform(key_list[3], (LEVELS,), jnp.float32, 0.99, 0.999), 0.99, 0.999),
        "decay_index": place_ends(jax.random.randint(key_list[4], (C,), 0, LEVELS), jax.random.fold_in(key_list[4], 1), 0, LEVELS - 1).astype(jnp.int32),
    }


def convolve(source, weight):
    padded = jnp.pad(source, ((0, 0), (1, 1), (1, 1), (0, 0)))
    height = source.shape[1]
    width = source.shape[2]
    depth = weight.shape[2]

    def one_frame(image):
        total = jnp.zeros((height * width, weight.shape[3]), jnp.float32)
        for tap_row in range(3):
            for tap_col in range(3):
                window = image[tap_row:tap_row + height, tap_col:tap_col + width, :].reshape(-1, depth)
                total = total + jnp.dot(window, weight[tap_row, tap_col], preferred_element_type=jnp.float32)
        return total.reshape(height, width, weight.shape[3])

    return lax.map(one_frame, padded)


def reference(latents, weight_in, weight_out, decay_table, decay_index):
    decays = decay_table[decay_index.astype(jnp.int32)]
    driven = convolve(latents, weight_in)

    def advance(running, incoming):
        running = decays * running + incoming
        return running, running

    start = jnp.zeros(latents.shape[1:], jnp.float32)
    _, states = lax.scan(advance, start, driven)
    rounded = states.astype(jnp.bfloat16)
    mixed = convolve(rounded, weight_out)
    return (latents.astype(jnp.float32) + jax.nn.gelu(mixed)).astype(jnp.bfloat16)
```

```python
import functools

import jax
import jax.numpy as jnp
from jax import lax
from jax.experimental import pallas as pl
from jax.experimental.pallas import tpu as pltpu
from jax.sharding import PartitionSpec as P

MESH = pl.DeviceIdType.MESH
PIECES = 4


def kernel(
    positions,
    strips,
    lat_hbm,
    win_hbm,
    wout_hbm,
    table_hbm,
    index_hbm,
    out_hbm,
    lat,
    win,
    wout,
    wide,
    partial,
    share,
    shared,
    carry,
    passed,
    relayed,
    mixed,
    table_ref,
    index_ref,
    wide_states,
    result,
    lat_sem,
    win_sem,
    wout_sem,
    small_sem,
    store_sem,
    share_send,
    share_recv,
    carry_send,
    carry_recv,
    relay_send,
    relay_recv,
    turn,
):
    frames, strip, width, channels = lat.shape
    row = lax.axis_index("rows")
    moment = lax.axis_index("tm")
    odd = lax.rem(row, 2)
    span = width // PIECES
    bottom = strip - 1
    final = frames - 1
    edge = (0, bottom)
    ghost = (strip, strip + 1)
    near = (row - 1 + 2 * odd, row + 1 - 2 * odd)
    has = tuple(jnp.logical_and(at >= 0, at < strips) for at in near)
    paired = strips % 2 == 0
    depth = 3 * channels
    has_before, has_after = moment > 0, moment < positions - 1

    def guard(side):
        if side == 1 and paired:
            return lambda act: act()
        return pl.when(has[side])

    def place(i, count):
        return i + odd * (count - 1 - 2 * i)

    barrier = pltpu.get_barrier_semaphore()
    greeted = (
        (has[0], {"rows": near[0]}),
        (has[1], {"rows": near[1]}),
        (has_before, {"tm": moment - 1}),
        (has_after, {"tm": moment + 1}),
    )
    total = 0
    for exists, where in greeted:
        total = total + exists.astype(jnp.int32)

        @pl.when(exists)
        def _():
            pl.semaphore_signal(barrier, inc=1, device_id=where, device_id_type=MESH)

    def load_lat(i):
        return pltpu.make_async_copy(lat_hbm.at[:, place(i, strip)], lat.at[:, i], lat_sem.at[i])

    def load_win(tap):
        return pltpu.make_async_copy(win_hbm.at[place(tap, 3)], win.at[pl.ds(tap * depth, depth)], win_sem.at[tap])

    def load_wout(tap):
        return pltpu.make_async_copy(wout_hbm.at[place(tap, 3)], wout.at[pl.ds(tap * depth, depth)], wout_sem.at[tap])

    load_table = pltpu.make_async_copy(table_hbm, table_ref, small_sem.at[0])
    load_index = pltpu.make_async_copy(index_hbm, index_ref, small_sem.at[1])

    load_table.start()
    load_index.start()
    for i in range(strip):
        load_lat(i).start()
    for tap in range(3):
        load_win(tap).start()

    def share_copy(side, kind, frame):
        return pltpu.make_async_remote_copy(
            src_ref=share.at[side, kind, frame],
            dst_ref=shared.at[side, kind, frame],
            send_sem=share_send.at[side, kind, frame],
            recv_sem=share_recv.at[side, kind, frame],
            device_id={"rows": near[side]},
            device_id_type=MESH,
        )

    def relay_copy():
        return pltpu.make_async_remote_copy(
            src_ref=carry.at[bottom],
            dst_ref=relayed,
            send_sem=relay_send,
            recv_sem=relay_recv,
            device_id={"rows": near[1]},
            device_id_type=MESH,
        )

    def carry_copy(i, piece):
        part = pl.ds(piece * span, span)
        return pltpu.make_async_remote_copy(
            src_ref=passed.at[i, part],
            dst_ref=carry.at[i, part],
            send_sem=carry_send.at[i, piece],
            recv_sem=carry_recv.at[i, piece],
            device_id={"tm": moment + 1},
            device_id_type=MESH,
        )

    column = lax.broadcasted_iota(jnp.int32, (width, channels), 0)

    def spread(value):
        full = value.astype(jnp.float32)
        before = jnp.where(column == 0, 0.0, pltpu.roll(full, 1, 0))
        after = jnp.where(column == width - 1, 0.0, pltpu.roll(full, width - 1, 0))
        middle = value.astype(jnp.bfloat16)
        return jnp.concatenate([before.astype(jnp.bfloat16), middle, after.astype(jnp.bfloat16)], axis=-1)

    def prepare(i):
        load_lat(i).wait()
        for frame in range(frames):
            wide[i, frame] = spread(lat[frame, i])

    def times(rows, weights, taps):
        window = [r.reshape(frames * width, 3 * channels) for r in rows]
        window = window[0] if len(rows) == 1 else jnp.concatenate(window, axis=-1)
        factor = weights[taps[0] * depth : (taps[-1] + 1) * depth]
        value = jnp.dot(window, factor, preferred_element_type=jnp.float32)
        return value.reshape(frames, width, channels)

    def scan(value):
        running = [value[0]]
        for frame in range(1, frames):
            running.append(decays * running[-1] + value[frame])
        return running

    def drive(i):
        taps = [tap for tap in range(3) if 0 <= i + tap - 1 < strip]
        states = scan(times([wide[i + tap - 1] for tap in taps], win, taps))
        for frame in range(frames):
            partial[i, frame] = states[frame]
            if i in edge:
                share[edge.index(i), 1, frame] = states[frame].astype(jnp.bfloat16)

    def offer(side):
        states = scan(times([wide[edge[side]]], win, [2 - 2 * side]))
        for frame in range(frames):
            partial[ghost[side], frame] = states[frame]
            share[side, 0, frame] = states[frame].astype(jnp.bfloat16)

    def send(side):
        @guard(side)
        def _():
            for frame in reversed(range(frames)):
                for kind in range(2):
                    share_copy(side, kind, frame).start()

    def absorb(side, which, kinds=(0, 1)):
        for frame in which:
            for kind in kinds:
                share_copy(side, kind, frame).wait_recv()
                i = (edge, ghost)[kind][side]
                partial[i, frame] = partial[i, frame] + shared[side, kind, frame].astype(jnp.float32)

    def block(act):
        pl.when(row >= 0)(act)

    def begin(i, pieces=range(PIECES)):
        for piece in pieces:
            part = pl.ds(piece * span, span)
            passed[i, part] = partial[i, final, part].astype(passed.dtype)
            carry_copy(i, piece).start()

    def advance(i, piece, last):
        part = pl.ds(piece * span, span)
        carry_copy(i, piece).wait_recv()
        if not last:
            value = partial[i, final, part] + growth[final] * carry[i, part].astype(jnp.float32)
            passed[i, part] = value.astype(passed.dtype)
            carry_copy(i, piece).start()

    def sent(i, pieces=range(PIECES)):
        for piece in pieces:
            carry_copy(i, piece).wait_send()

    def stretch(i, carried):
        if carried:
            arrived = (relayed[...] if i == ghost[1] else carry[i]).astype(jnp.float32)
        for frame in range(frames):
            state = partial[i, frame]
            if carried:
                state = state + growth[frame] * arrived
            wide_states[i, frame] = spread(state)

    def product(sources, i):
        taps = [source - i + 1 for source in sources]
        return times([wide_states[source] for source in sources], wout, taps)

    def write(i, value):
        for frame in range(frames):
            updated = lat[frame, i].astype(jnp.float32) + jax.nn.gelu(value[frame])
            result[frame, i] = updated.astype(jnp.bfloat16)
        store(i).start()

    def store(i):
        return pltpu.make_async_copy(result.at[:, i], out_hbm.at[:, place(i, strip)], store_sem.at[i])

    def reach(side):
        return times([wide_states[ghost[side]]], wout, [2 * side])

    def wait_wout():
        for tap in range(3):
            load_wout(tap).wait()

    for i in range(strip):
        prepare(i)
    load_table.wait()
    load_index.wait()
    chosen = index_ref[...]
    decays = jnp.zeros(chosen.shape, jnp.float32)
    for level in range(table_ref.shape[0]):
        decays = jnp.where(chosen == level, table_ref[level], decays)
    growth = [decays]
    for _ in range(frames - 1):
        growth.append(growth[-1] * decays)

    for tap in range(3):
        load_win(tap).wait()
    for tap in range(3):
        load_wout(tap).start()

    middle = list(range(1, bottom))
    first, late = middle[0], middle[1:]

    @block
    def _():
        drive(first)

    pl.semaphore_wait(barrier, total)

    @pl.when(jnp.logical_not(has_before))
    def _():
        if positions > 1:
            begin(first)

    @block
    def _():
        offer(0)
        drive(0)

    send(0)

    @block
    def _():
        for i in late:
            drive(i)
        offer(1)
        drive(bottom)

    send(1)

    def start():
        def far():
            absorb(0, [final], [0])
            if positions > 1:
                begin(0)
            absorb(0, [final], [1])
            if positions > 1:
                begin(ghost[0])

        def lead():
            if positions > 1:
                for i in late:
                    begin(i)

            @guard(1)
            def _():
                absorb(1, [final], [0])

            if positions > 1:
                begin(bottom)

            def pass_turn():
                @guard(1)
                def _():
                    pl.semaphore_signal(turn, inc=1, device_id={"rows": near[1]}, device_id_type=MESH)

            @pl.when(has[0])
            def _():
                far()
                if positions > 1:
                    for i in [*middle, bottom, 0]:
                        sent(i)
                    pass_turn()
                    sent(ghost[0])

            @pl.when(jnp.logical_not(has[0]))
            def _():
                if positions > 1:
                    begin(0)
                    for i in [*middle, bottom]:
                        sent(i)
                    pass_turn()
                    sent(0)

        def second():
            if positions > 1:
                for i in late:
                    begin(i)
            absorb(1, [final], [0])
            if positions > 1:
                pl.semaphore_wait(turn, 1)
                begin(bottom)

            @pl.when(has[0])
            def _():
                far()

            if positions > 1:

                @pl.when(jnp.logical_not(has[0]))
                def _():
                    begin(0)

        @pl.when(odd == 0)
        def _():
            lead()

        @pl.when(odd == 1)
        def _():
            second()

        @guard(1)
        def _():
            absorb(1, [final], [1])
            absorb(1, range(final))

        wait_wout()

        @block
        def _():
            for i in range(1, strip):
                stretch(i, False)
            for i in range(2, bottom):
                write(i, product([i - 1, i, i + 1], i))
            if paired:
                stretch(ghost[1], False)
                write(bottom, product([bottom - 1, bottom], bottom) + reach(1))
            else:
                mixed[bottom] = product([bottom - 1, bottom], bottom)

        if not paired:

            @pl.when(has[1])
            def _():
                stretch(ghost[1], False)
                mixed[bottom] = mixed[bottom] + reach(1)

            write(bottom, mixed[bottom])

        @pl.when(has[0])
        def _():
            absorb(0, range(final))

        @block
        def _():
            stretch(0, False)
            write(1, product([0, 1, 2], 1))
            mixed[0] = product([0, 1], 0)

        @pl.when(has[0])
        def _():
            stretch(ghost[0], False)
            mixed[0] = mixed[0] + reach(0)

        write(0, mixed[0])

    def follow(last):
        def receive(i, pieces=range(PIECES)):
            for piece in pieces:
                advance(i, piece, last)

        def receive_ghost():
            @pl.when(has[0])
            def _():
                absorb(0, [final], [1])
                receive(ghost[0])

        def first_rows():
            stretch(first, True)
            for i in range(first + 2):
                mixed[i] = product([first], i)

        def late_rows():
            for i in late:
                stretch(i, True)
                mixed[i + 1] = product([i], i + 1)
                mixed[i - 1] = mixed[i - 1] + product([i], i - 1)
                mixed[i] = mixed[i] + product([i], i)

        def bottom_rows():
            stretch(bottom, True)
            mixed[bottom] = mixed[bottom] + product([bottom], bottom)
            mixed[bottom - 1] = mixed[bottom - 1] + product([bottom], bottom - 1)
            for i in range(2, bottom):
                write(i, mixed[i])

        def far_rest():
            @pl.when(has[0])
            def _():
                absorb(0, range(final))

        def top_rows():
            stretch(0, True)
            mixed[0] = mixed[0] + product([0], 0)
            write(1, mixed[1] + product([0], 1))

        def core_rows():
            if paired:
                relay_copy().wait_recv()

                @block
                def _():
                    stretch(ghost[1], True)
                    write(bottom, mixed[bottom] + reach(1))
            else:

                @pl.when(has[1])
                def _():
                    relay_copy().wait_recv()
                    stretch(ghost[1], True)
                    mixed[bottom] = mixed[bottom] + reach(1)

                write(bottom, mixed[bottom])

        def early(act):
            (block if last else pl.when(odd == 1))(act)

        def later(act):
            if not last:
                pl.when(odd == 0)(act)

        wait_wout()
        receive(first)
        if last:
            block(first_rows)
        for i in late:
            receive(i)
        if not last:
            early(first_rows)
        early(late_rows)

        @guard(1)
        def _():
            absorb(1, reversed(range(frames)))

        receive(bottom)

        @guard(1)
        def _():
            relay_copy().start()

        if last:
            block(bottom_rows)
            pl.when(odd == 1)(core_rows)

        @pl.when(has[0])
        def _():
            absorb(0, [final], [0])

        receive(0)
        if last:
            far_rest()
            block(top_rows)
            pl.when(odd == 0)(core_rows)
            receive_ghost()
        else:
            receive_ghost()
            later(first_rows)
            later(late_rows)
            block(bottom_rows)
            core_rows()
            far_rest()
            block(top_rows)

        @pl.when(has[0])
        def _():
            stretch(ghost[0], True)
            write(0, mixed[0] + reach(0))

        @pl.when(jnp.logical_not(has[0]))
        def _():
            write(0, mixed[0])

    @pl.when(jnp.logical_not(has_before))
    def _():
        start()

    @pl.when(jnp.logical_and(has_before, has_after))
    def _():
        follow(False)

    @pl.when(jnp.logical_and(has_before, jnp.logical_not(has_after)))
    def _():
        follow(True)

    for side in range(2):

        @pl.when(has[side])
        def _():
            for kind in range(2):
                for frame in range(frames):
                    share_copy(side, kind, frame).wait_send()

    @pl.when(jnp.logical_and(has[1], has_before))
    def _():
        relay_copy().wait_send()

    pending = jnp.logical_and(has_after, jnp.logical_or(has_before, odd == 1))

    @pl.when(pending)
    def _():
        for i in range(strip):
            sent(i)

    @pl.when(jnp.logical_and(has[0], pending))
    def _():
        sent(ghost[0])

    for i in range(strip):
        store(i).wait()


def local(positions, strips, latents, weight_in, weight_out, decay_table, decay_index):
    frames, strip, width, channels = latents.shape
    link = jnp.bfloat16 if positions <= 8 else jnp.float32
    half = jnp.bfloat16
    dma = pltpu.SemaphoreType.DMA
    anywhere = pl.BlockSpec(memory_space=pl.ANY)
    return pl.pallas_call(
        functools.partial(kernel, positions, strips),
        out_shape=jax.ShapeDtypeStruct(latents.shape, latents.dtype),
        in_specs=[anywhere] * 5,
        out_specs=anywhere,
        scratch_shapes=[
            pltpu.VMEM((frames, strip, width, channels), half),
            pltpu.VMEM((9 * channels, channels), half),
            pltpu.VMEM((9 * channels, channels), half),
            pltpu.VMEM((strip, frames, width, 3 * channels), half),
            pltpu.VMEM((strip + 2, frames, width, channels), jnp.float32),
            pltpu.VMEM((2, 2, frames, width, channels), half),
            pltpu.VMEM((2, 2, frames, width, channels), half),
            pltpu.VMEM((strip + 1, width, channels), link),
            pltpu.VMEM((strip + 1, width, channels), link),
            pltpu.VMEM((width, channels), link),
            pltpu.VMEM((strip, frames, width, channels), jnp.float32),
            pltpu.SMEM(decay_table.shape, jnp.float32),
            pltpu.VMEM((1, channels), jnp.int32),
            pltpu.VMEM((strip + 2, frames, width, 3 * channels), half),
            pltpu.VMEM((frames, strip, width, channels), half),
            dma((strip,)),
            dma((3,)),
            dma((3,)),
            dma((2,)),
            dma((strip,)),
            dma((2, 2, frames)),
            dma((2, 2, frames)),
            dma((strip + 1, PIECES)),
            dma((strip + 1, PIECES)),
            dma,
            dma,
            pltpu.SemaphoreType.REGULAR,
        ],
        compiler_params=pltpu.CompilerParams(collective_id=0, has_side_effects=True, vmem_limit_bytes=32 * 1024 * 1024),
    )(
        pltpu.with_memory_space_constraint(latents, pltpu.HBM),
        pltpu.with_memory_space_constraint(weight_in.reshape(3, 3 * channels, channels), pltpu.HBM),
        pltpu.with_memory_space_constraint(weight_out.reshape(3, 3 * channels, channels), pltpu.HBM),
        pltpu.with_memory_space_constraint(decay_table, pltpu.HBM),
        pltpu.with_memory_space_constraint(decay_index.reshape(1, channels), pltpu.HBM),
    )


def solution(mesh):
    in_specs = (P(("groups", "tm"), "rows", None, None), P(), P(), P(), P())
    out_specs = P(("groups", "tm"), "rows", None, None)
    body = functools.partial(local, mesh.shape["tm"], mesh.shape["rows"])
    return jax.shard_map(body, mesh=mesh, in_specs=in_specs, out_specs=out_specs, check_vma=False)
```

```python
import functools
import math

import jax
import jax.numpy as jnp
from jax import lax
from jax.experimental import pallas as pl
from jax.experimental.pallas import tpu as pltpu
from jax.sharding import PartitionSpec as P

MESH = pl.DeviceIdType.MESH
PIECES = 4
ROOT = (2.0 / math.pi) ** 0.5
CUBIC = 0.044715 * ROOT


def kernel(
    positions,
    strips,
    lat_hbm,
    win_hbm,
    wout_hbm,
    table_hbm,
    index_hbm,
    out_hbm,
    lat,
    win,
    wout,
    wide,
    partial,
    share,
    shared,
    carry,
    passed,
    relayed,
    mixed,
    table_ref,
    index_ref,
    wide_states,
    result,
    lat_sem,
    win_sem,
    wout_sem,
    small_sem,
    store_sem,
    share_send,
    share_recv,
    carry_send,
    carry_recv,
    relay_send,
    relay_recv,
    turn,
):
    frames, strip, width, channels = lat.shape
    row = lax.axis_index("rows")
    moment = lax.axis_index("tm")
    odd = lax.rem(row, 2)
    span = width // PIECES
    bottom = strip - 1
    final = frames - 1
    edge = (0, bottom)
    ghost = (strip, strip + 1)
    near = (row - 1 + 2 * odd, row + 1 - 2 * odd)
    has = tuple(jnp.logical_and(at >= 0, at < strips) for at in near)
    paired = strips % 2 == 0
    depth = 3 * channels
    has_before, has_after = moment > 0, moment < positions - 1

    def guard(side):
        if side == 1 and paired:
            return lambda act: act()
        return pl.when(has[side])

    def place(i, count):
        return i + odd * (count - 1 - 2 * i)

    def load_lat(i):
        return pltpu.make_async_copy(lat_hbm.at[:, place(i, strip)], lat.at[:, i], lat_sem.at[i])

    def load_win(tap):
        return pltpu.make_async_copy(win_hbm.at[place(tap, 3)], win.at[pl.ds(tap * depth, depth)], win_sem.at[tap])

    def load_wout(tap):
        return pltpu.make_async_copy(wout_hbm.at[place(tap, 3)], wout.at[tap], wout_sem)

    load_table = pltpu.make_async_copy(table_hbm, table_ref, small_sem.at[0])
    load_index = pltpu.make_async_copy(index_hbm, index_ref, small_sem.at[1])

    for i in range(3):
        load_lat(i).start()
    load_win(0).start()

    barrier = pltpu.get_barrier_semaphore()
    greeted = (
        (has[0], {"rows": near[0]}),
        (has[1], {"rows": near[1]}),
        (has_before, {"tm": moment - 1}),
        (has_after, {"tm": moment + 1}),
    )
    total = 0
    for exists, where in greeted:
        total = total + exists.astype(jnp.int32)

        @pl.when(exists)
        def _():
            pl.semaphore_signal(barrier, inc=1, device_id=where, device_id_type=MESH)

    load_table.start()
    load_index.start()
    for tap in range(1, 3):
        load_win(tap).start()
    for i in range(3, strip):
        load_lat(i).start()

    def share_copy(side, kind, frame):
        return pltpu.make_async_remote_copy(
            src_ref=share.at[side, frame, kind],
            dst_ref=shared.at[side, frame, kind],
            send_sem=share_send.at[side],
            recv_sem=share_recv.at[side, kind if frame == final else 2],
            device_id={"rows": near[side]},
            device_id_type=MESH,
        )

    def relay_copy():
        return pltpu.make_async_remote_copy(
            src_ref=carry.at[bottom],
            dst_ref=relayed,
            send_sem=relay_send,
            recv_sem=relay_recv,
            device_id={"rows": near[1]},
            device_id_type=MESH,
        )

    def carry_copy(i, piece):
        part = pl.ds(piece * span, span)
        return pltpu.make_async_remote_copy(
            src_ref=passed.at[i, part],
            dst_ref=carry.at[i, part],
            send_sem=carry_send.at[min(i, 1) if i < strip else 2],
            recv_sem=carry_recv.at[i, piece],
            device_id={"tm": moment + 1},
            device_id_type=MESH,
        )

    column = lax.broadcasted_iota(jnp.int32, (width, channels), 0)

    def spread(value):
        full = value.astype(jnp.float32)
        before = jnp.where(column == 0, 0.0, pltpu.roll(full, 1, 0))
        after = jnp.where(column == width - 1, 0.0, pltpu.roll(full, width - 1, 0))
        middle = value.astype(jnp.bfloat16)
        return jnp.concatenate([before.astype(jnp.bfloat16), middle, after.astype(jnp.bfloat16)], axis=-1)

    def prepare(i):
        for frame in range(frames):
            wide[i, frame] = spread(lat[frame, i])

    def times(rows, weights, taps):
        window = [r.reshape(frames * width, 3 * channels) for r in rows]
        window = window[0] if len(rows) == 1 else jnp.concatenate(window, axis=-1)
        if len(weights.shape) == 3:
            factor = weights[taps[0] : taps[-1] + 1].reshape(len(taps) * depth, channels)
        else:
            factor = weights[taps[0] * depth : (taps[-1] + 1) * depth]
        value = jnp.dot(window, factor, preferred_element_type=jnp.float32)
        return value.reshape(frames, width, channels)

    def scan(value):
        running = [value[0]]
        for frame in range(1, frames):
            running.append(decays * running[-1] + value[frame])
        return running

    def drive(i):
        taps = [tap for tap in range(3) if 0 <= i + tap - 1 < strip]
        states = scan(times([wide[i + tap - 1] for tap in taps], win, taps))
        for frame in range(frames):
            partial[i, frame] = states[frame]
            if i in edge:
                share[edge.index(i), frame, 1] = states[frame].astype(jnp.bfloat16)

    def offer(side):
        states = scan(times([wide[edge[side]]], win, [2 - 2 * side]))
        for frame in range(frames):
            partial[ghost[side], frame] = states[frame]
            share[side, frame, 0] = states[frame].astype(jnp.bfloat16)

    def send(side):
        @guard(side)
        def _():
            for frame in reversed(range(frames)):
                for kind in range(2):
                    share_copy(side, kind, frame).start()

    def add_share(side, kind, frame):
        i = (edge, ghost)[kind][side]
        partial[i, frame] = partial[i, frame] + shared[side, frame, kind].astype(jnp.float32)

    def absorb(side, kind):
        share_copy(side, kind, final).wait_recv()
        add_share(side, kind, final)

    def absorb_rest(side):
        if final == 0:
            return
        part = pl.ds(0, final)
        pltpu.make_async_remote_copy(
            src_ref=share.at[side, part],
            dst_ref=shared.at[side, part],
            send_sem=share_send.at[side],
            recv_sem=share_recv.at[side, 2],
            device_id={"rows": near[side]},
            device_id_type=MESH,
        ).wait_recv()
        for frame in range(final):
            for kind in range(2):
                add_share(side, kind, frame)

    def share_sent(side):
        pltpu.make_async_remote_copy(
            src_ref=share.at[side],
            dst_ref=shared.at[side],
            send_sem=share_send.at[side],
            recv_sem=share_recv.at[side, 2],
            device_id={"rows": near[side]},
            device_id_type=MESH,
        ).wait_send()

    def block(act):
        pl.when(row >= 0)(act)

    def begin(i, pieces=range(PIECES)):
        for piece in pieces:
            part = pl.ds(piece * span, span)
            passed[i, part] = partial[i, final, part].astype(passed.dtype)
            carry_copy(i, piece).start()

    def advance(i, piece, last):
        part = pl.ds(piece * span, span)
        carry_copy(i, piece).wait_recv()
        if not last:
            value = partial[i, final, part] + growth[final] * carry[i, part].astype(jnp.float32)
            passed[i, part] = value.astype(passed.dtype)
            carry_copy(i, piece).start()

    def sent(group):
        part = (pl.ds(0, 1), pl.ds(1, strip - 1), pl.ds(strip, 1))[group]
        pltpu.make_async_remote_copy(
            src_ref=passed.at[part],
            dst_ref=carry.at[part],
            send_sem=carry_send.at[(0, 1, 2)[group]],
            recv_sem=carry_recv.at[0, 0],
            device_id={"tm": moment + 1},
            device_id_type=MESH,
        ).wait_send()

    def stretch(i, carried):
        if carried:
            arrived = (relayed[...] if i == ghost[1] else carry[i]).astype(jnp.float32)
        for frame in range(frames):
            state = partial[i, frame]
            if carried:
                state = state + growth[frame] * arrived
            wide_states[i, frame] = spread(state)

    def product(sources, i):
        taps = [source - i + 1 for source in sources]
        return times([wide_states[source] for source in sources], wout, taps)

    def write(i, value):
        for frame in range(frames):
            x = value[frame]
            half = 0.5 * x
            angle = x * (ROOT + CUBIC * (x * x))
            updated = lat[frame, i].astype(jnp.float32) + (half + half * jnp.tanh(angle))
            result[frame, i] = updated.astype(jnp.bfloat16)
        store(i).start()

    def store(i):
        return pltpu.make_async_copy(result.at[:, i], out_hbm.at[:, place(i, strip)], store_sem)

    def reach(side):
        return times([wide_states[ghost[side]]], wout, [2 * side])

    def wait_wout():
        pltpu.make_async_copy(wout_hbm, wout, wout_sem).wait()

    middle = list(range(1, bottom))
    first, late = middle[0], middle[1:]
    for i in range(3):
        load_lat(i).wait()
        prepare(i)
    load_table.wait()
    load_index.wait()
    chosen = index_ref[...]
    decays = jnp.zeros(chosen.shape, jnp.float32)
    for level in range(table_ref.shape[0]):
        decays = jnp.where(chosen == level, table_ref[level], decays)
    growth = [decays]
    for _ in range(frames - 1):
        growth.append(growth[-1] * decays)
    load_win(0).wait()

    @block
    def _():
        partial[first] = times([wide[0]], win, [0])

    load_win(1).wait()
    load_win(2).wait()

    @block
    def _():
        value = times([wide[1]], win, [1]) + times([wide[2]], win, [2])
        states = scan(partial[first] + value)
        for frame in range(frames):
            partial[first, frame] = states[frame]

    for i in range(3, strip):
        load_lat(i).wait()
        prepare(i)

    pl.semaphore_wait(barrier, total)

    leads = jnp.logical_and(jnp.logical_not(has_before), odd == 1)

    @pl.when(leads)
    def _():
        if positions > 1:
            begin(first)
        for i in late:
            drive(i)
            if positions > 1:
                begin(i)

    @block
    def _():
        offer(0)
        drive(0)

    send(0)

    @pl.when(jnp.logical_and(jnp.logical_not(has_before), odd == 0))
    def _():
        if positions > 1:
            begin(first)

    for tap in range(3):
        load_wout(tap).start()

    @pl.when(jnp.logical_not(leads))
    def _():
        for i in late:
            drive(i)
        offer(1)
        drive(bottom)

    @pl.when(leads)
    def _():
        offer(1)
        drive(bottom)

    send(1)

    def start():
        def far():
            absorb(0, 0)
            if positions > 1:
                begin(0)
            absorb(0, 1)
            if positions > 1:
                begin(ghost[0])

        def lead():
            if positions > 1:
                for i in late:
                    begin(i)

            @guard(1)
            def _():
                absorb(1, 0)

            if positions > 1:
                begin(bottom)

            def pass_turn():
                @guard(1)
                def _():
                    pl.semaphore_signal(turn, inc=1, device_id={"rows": near[1]}, device_id_type=MESH)

            @pl.when(has[0])
            def _():
                far()
                if positions > 1:
                    sent(1)
                    sent(0)
                    pass_turn()
                    sent(2)

            @pl.when(jnp.logical_not(has[0]))
            def _():
                if positions > 1:
                    begin(0)
                    sent(1)
                    pass_turn()
                    sent(0)

        def second():
            absorb(1, 0)
            if positions > 1:
                begin(bottom)
                pl.semaphore_wait(turn, 1)

            @pl.when(has[0])
            def _():
                far()

            if positions > 1:

                @pl.when(jnp.logical_not(has[0]))
                def _():
                    begin(0)

        @pl.when(odd == 0)
        def _():
            lead()

        @pl.when(odd == 1)
        def _():
            second()

        @guard(1)
        def _():
            absorb(1, 1)
            absorb_rest(1)

        wait_wout()

        @block
        def _():
            for i in range(1, strip):
                stretch(i, False)
            for i in range(2, bottom):
                write(i, product([i - 1, i, i + 1], i))
            if paired:
                stretch(ghost[1], False)
                write(bottom, product([bottom - 1, bottom], bottom) + reach(1))
            else:
                mixed[bottom] = product([bottom - 1, bottom], bottom)

        if not paired:

            @pl.when(has[1])
            def _():
                stretch(ghost[1], False)
                mixed[bottom] = mixed[bottom] + reach(1)

            write(bottom, mixed[bottom])

        @pl.when(has[0])
        def _():
            absorb_rest(0)

        @block
        def _():
            stretch(0, False)
            write(1, product([0, 1, 2], 1))
            mixed[0] = product([0, 1], 0)

        @pl.when(has[0])
        def _():
            stretch(ghost[0], False)
            mixed[0] = mixed[0] + reach(0)

        write(0, mixed[0])

    def follow(last):
        def receive(i, pieces=range(PIECES)):
            for piece in pieces:
                advance(i, piece, last)

        def receive_ghost():
            @pl.when(has[0])
            def _():
                absorb(0, 1)
                receive(ghost[0])

        def first_rows():
            stretch(first, True)
            for i in range(first + 2):
                mixed[i] = product([first], i)

        def late_rows():
            for i in late:
                stretch(i, True)
                mixed[i + 1] = product([i], i + 1)
                mixed[i - 1] = mixed[i - 1] + product([i], i - 1)
                mixed[i] = mixed[i] + product([i], i)

        def bottom_rows(done=False):
            stretch(bottom, True)
            mixed[bottom] = mixed[bottom] + product([bottom], bottom)
            mixed[bottom - 1] = mixed[bottom - 1] + product([bottom], bottom - 1)
            for i in range(2, bottom):
                write(i, mixed[i])
            if done:
                write(bottom, mixed[bottom])

        def far_rest():
            @pl.when(has[0])
            def _():
                absorb_rest(0)

        def top_rows():
            stretch(0, True)
            mixed[0] = mixed[0] + product([0], 0)
            write(1, mixed[1] + product([0], 1))

        def core_rows():
            @guard(1)
            def _():
                relay_copy().wait_recv()

                @block
                def _():
                    stretch(ghost[1], True)
                    mixed[bottom] = mixed[bottom] + reach(1)

        waits = jnp.logical_and(has[0], odd == 1)

        def core_close():
            if paired:
                relay_copy().wait_recv()
                stretch(ghost[1], True)
                write(bottom, mixed[bottom] + reach(1))
            else:
                core_rows()
                write(bottom, mixed[bottom])

        def ghost_rows():
            @pl.when(has[0])
            def _():
                stretch(ghost[0], True)
                write(0, mixed[0] + reach(0))

            @pl.when(jnp.logical_not(has[0]))
            def _():
                write(0, mixed[0])

        def early(act):
            (block if last else pl.when(odd == 1))(act)

        def later(act):
            if not last:
                pl.when(odd == 0)(act)

        wait_wout()
        receive(first)
        if last:
            block(first_rows)
        for i in late:
            receive(i)
        if not last:
            early(first_rows)
        early(late_rows)

        @guard(1)
        def _():
            absorb(1, 0)
            absorb(1, 1)
            absorb_rest(1)

        receive(bottom)

        @guard(1)
        def _():
            relay_copy().start()

        if last:

            block(bottom_rows)

            pl.when(jnp.logical_not(waits))(core_close)

        @pl.when(has[0])
        def _():
            absorb(0, 0)

        receive(0)
        if last:
            far_rest()
            block(top_rows)
            pl.when(waits)(core_close)
            receive_ghost()
            ghost_rows()
        else:
            receive_ghost()
            later(first_rows)
            later(late_rows)
            core_rows()
            block(lambda: bottom_rows(True))
            far_rest()
            block(top_rows)
            ghost_rows()

    @pl.when(jnp.logical_not(has_before))
    def _():
        start()

    @pl.when(jnp.logical_and(has_before, has_after))
    def _():
        follow(False)

    @pl.when(jnp.logical_and(has_before, jnp.logical_not(has_after)))
    def _():
        follow(True)

    for side in range(2):

        @pl.when(has[side])
        def _():
            share_sent(side)

    @pl.when(jnp.logical_and(has[1], has_before))
    def _():
        relay_copy().wait_send()

    pending = jnp.logical_and(has_after, jnp.logical_or(has_before, odd == 1))

    @pl.when(pending)
    def _():
        sent(1)
        sent(0)

    @pl.when(jnp.logical_and(has[0], pending))
    def _():
        sent(2)

    pltpu.make_async_copy(result, out_hbm, store_sem).wait()


def local(positions, strips, latents, weight_in, weight_out, decay_table, decay_index):
    frames, strip, width, channels = latents.shape
    link = jnp.bfloat16 if positions <= 8 else jnp.float32
    half = jnp.bfloat16
    dma = pltpu.SemaphoreType.DMA
    anywhere = pl.BlockSpec(memory_space=pl.ANY)
    return pl.pallas_call(
        functools.partial(kernel, positions, strips),
        out_shape=jax.ShapeDtypeStruct(latents.shape, latents.dtype),
        in_specs=[anywhere] * 5,
        out_specs=anywhere,
        scratch_shapes=[
            pltpu.VMEM((frames, strip, width, channels), half),
            pltpu.VMEM((9 * channels, channels), half),
            pltpu.VMEM((3, 3 * channels, channels), half),
            pltpu.VMEM((strip, frames, width, 3 * channels), half),
            pltpu.VMEM((strip + 2, frames, width, channels), jnp.float32),
            pltpu.VMEM((2, frames, 2, width, channels), half),
            pltpu.VMEM((2, frames, 2, width, channels), half),
            pltpu.VMEM((strip + 1, width, channels), link),
            pltpu.VMEM((strip + 1, width, channels), link),
            pltpu.VMEM((width, channels), link),
            pltpu.VMEM((strip, frames, width, channels), jnp.float32),
            pltpu.SMEM(decay_table.shape, jnp.float32),
            pltpu.VMEM((1, channels), jnp.int32),
            pltpu.VMEM((strip + 2, frames, width, 3 * channels), half),
            pltpu.VMEM((frames, strip, width, channels), half),
            dma((strip,)),
            dma((3,)),
            dma,
            dma((2,)),
            dma,
            dma((2,)),
            dma((2, 3)),
            dma((3,)),
            dma((strip + 1, PIECES)),
            dma,
            dma,
            pltpu.SemaphoreType.REGULAR,
        ],
        compiler_params=pltpu.CompilerParams(collective_id=0, has_side_effects=True, vmem_limit_bytes=32 * 1024 * 1024),
    )(
        pltpu.with_memory_space_constraint(latents, pltpu.HBM),
        pltpu.with_memory_space_constraint(weight_in.reshape(3, 3 * channels, channels), pltpu.HBM),
        pltpu.with_memory_space_constraint(weight_out.reshape(3, 3 * channels, channels), pltpu.HBM),
        pltpu.with_memory_space_constraint(decay_table, pltpu.HBM),
        pltpu.with_memory_space_constraint(decay_index.reshape(1, channels), pltpu.HBM),
    )


def solution(mesh):
    in_specs = (P(("groups", "tm"), "rows", None, None), P(), P(), P(), P())
    out_specs = P(("groups", "tm"), "rows", None, None)
    body = functools.partial(local, mesh.shape["tm"], mesh.shape["rows"])
    return jax.shard_map(body, mesh=mesh, in_specs=in_specs, out_specs=out_specs, check_vma=False)
```

```python
import functools
import math

import jax
import jax.numpy as jnp
from jax import lax
from jax.experimental import pallas as pl
from jax.experimental.pallas import tpu as pltpu
from jax.sharding import PartitionSpec as P

MESH = pl.DeviceIdType.MESH
PIECES = 4
ROOT = (2.0 / math.pi) ** 0.5
CUBIC = 0.044715 * ROOT


def kernel(
    positions,
    strips,
    lat_hbm,
    win_hbm,
    wout_hbm,
    table_hbm,
    index_hbm,
    out,
    lat,
    win,
    wout,
    wide,
    partial,
    share,
    shared,
    carry,
    passed,
    relayed,
    mixed,
    table_ref,
    index_ref,
    wide_states,
    lat_sem,
    win_sem,
    wout_sem,
    small_sem,
    share_send,
    share_recv,
    carry_send,
    carry_recv,
    relay_send,
    relay_recv,
    turn,
):
    frames, strip, width, channels = lat.shape
    row = lax.axis_index("rows")
    moment = lax.axis_index("tm")
    odd = lax.rem(row, 2)
    span = width // PIECES
    bottom = strip - 1
    final = frames - 1
    edge = (0, bottom)
    ghost = (strip, strip + 1)
    near = (row - 1 + 2 * odd, row + 1 - 2 * odd)
    has = tuple(jnp.logical_and(at >= 0, at < strips) for at in near)
    paired = strips % 2 == 0
    depth = 3 * channels
    has_before, has_after = moment > 0, moment < positions - 1

    def guard(side):
        if side == 1 and paired:
            return lambda act: act()
        return pl.when(has[side])

    def place(i, count):
        return i + odd * (count - 1 - 2 * i)

    def load_lat(i):
        return pltpu.make_async_copy(lat_hbm.at[:, place(i, strip)], lat.at[:, i], lat_sem.at[0 if i < 3 else 1])

    def load_win(tap):
        return pltpu.make_async_copy(win_hbm.at[place(tap, 3)], win.at[pl.ds(tap * depth, depth)], win_sem.at[tap])

    def load_wout(tap):
        return pltpu.make_async_copy(wout_hbm.at[place(tap, 3)], wout.at[tap], wout_sem)

    load_table = pltpu.make_async_copy(table_hbm, table_ref, small_sem.at[0])
    load_index = pltpu.make_async_copy(index_hbm, index_ref, small_sem.at[1])

    for i in range(3):
        load_lat(i).start()
    load_win(0).start()

    barrier = pltpu.get_barrier_semaphore()
    greeted = (
        (has[0], {"rows": near[0]}),
        (has[1], {"rows": near[1]}),
        (has_before, {"tm": moment - 1}),
        (has_after, {"tm": moment + 1}),
    )
    total = 0
    for exists, where in greeted:
        total = total + exists.astype(jnp.int32)

        @pl.when(exists)
        def _():
            pl.semaphore_signal(barrier, inc=1, device_id=where, device_id_type=MESH)

    load_table.start()
    load_index.start()
    for tap in range(1, 3):
        load_win(tap).start()
    for i in range(3, strip):
        load_lat(i).start()

    def share_copy(side, kind, frame):
        return pltpu.make_async_remote_copy(
            src_ref=share.at[side, frame, kind],
            dst_ref=shared.at[side, frame, kind],
            send_sem=share_send.at[side],
            recv_sem=share_recv.at[side, kind if frame == final else 2],
            device_id={"rows": near[side]},
            device_id_type=MESH,
        )

    def relay_copy():
        return pltpu.make_async_remote_copy(
            src_ref=carry.at[bottom],
            dst_ref=relayed,
            send_sem=relay_send,
            recv_sem=relay_recv,
            device_id={"rows": near[1]},
            device_id_type=MESH,
        )

    def carry_copy(i, piece):
        part = pl.ds(piece * span, span)
        return pltpu.make_async_remote_copy(
            src_ref=passed.at[i, part],
            dst_ref=carry.at[i, part],
            send_sem=carry_send.at[min(i, 1) if i < strip else 2],
            recv_sem=carry_recv.at[i, piece],
            device_id={"tm": moment + 1},
            device_id_type=MESH,
        )

    column = lax.broadcasted_iota(jnp.int32, (width, channels), 0)

    def spread(value):
        full = value.astype(jnp.float32)
        before = jnp.where(column == 0, 0.0, pltpu.roll(full, 1, 0))
        after = jnp.where(column == width - 1, 0.0, pltpu.roll(full, width - 1, 0))
        middle = value.astype(jnp.bfloat16)
        return jnp.concatenate([before.astype(jnp.bfloat16), middle, after.astype(jnp.bfloat16)], axis=-1)

    def prepare(i):
        for frame in range(frames):
            wide[i, frame] = spread(lat[frame, i])

    def times(rows, weights, taps):
        window = [r.reshape(frames * width, 3 * channels) for r in rows]
        window = window[0] if len(rows) == 1 else jnp.concatenate(window, axis=-1)
        if len(weights.shape) == 3:
            factor = weights[taps[0] : taps[-1] + 1].reshape(len(taps) * depth, channels)
        else:
            factor = weights[taps[0] * depth : (taps[-1] + 1) * depth]
        value = jnp.dot(window, factor, preferred_element_type=jnp.float32)
        return value.reshape(frames, width, channels)

    def scan(value):
        running = [value[0]]
        for frame in range(1, frames):
            running.append(decays * running[-1] + value[frame])
        return running

    def drive(i):
        taps = [tap for tap in range(3) if 0 <= i + tap - 1 < strip]
        states = scan(times([wide[i + tap - 1] for tap in taps], win, taps))
        for frame in range(frames):
            partial[i, frame] = states[frame]
            if i in edge:
                share[edge.index(i), frame, 1] = states[frame].astype(jnp.bfloat16)

    def offer(side):
        states = scan(times([wide[edge[side]]], win, [2 - 2 * side]))
        for frame in range(frames):
            partial[ghost[side], frame] = states[frame]
            share[side, frame, 0] = states[frame].astype(jnp.bfloat16)

    def send(side):
        @guard(side)
        def _():
            for frame in reversed(range(frames)):
                for kind in range(2):
                    share_copy(side, kind, frame).start()

    def add_share(side, kind, frame):
        i = (edge, ghost)[kind][side]
        partial[i, frame] = partial[i, frame] + shared[side, frame, kind].astype(jnp.float32)

    def absorb(side, kind):
        share_copy(side, kind, final).wait_recv()
        add_share(side, kind, final)

    def absorb_rest(side):
        if final == 0:
            return
        part = pl.ds(0, final)
        pltpu.make_async_remote_copy(
            src_ref=share.at[side, part],
            dst_ref=shared.at[side, part],
            send_sem=share_send.at[side],
            recv_sem=share_recv.at[side, 2],
            device_id={"rows": near[side]},
            device_id_type=MESH,
        ).wait_recv()
        for frame in range(final):
            for kind in range(2):
                add_share(side, kind, frame)

    def share_sent(side):
        pltpu.make_async_remote_copy(
            src_ref=share.at[side],
            dst_ref=shared.at[side],
            send_sem=share_send.at[side],
            recv_sem=share_recv.at[side, 2],
            device_id={"rows": near[side]},
            device_id_type=MESH,
        ).wait_send()

    def block(act):
        pl.when(row >= 0)(act)

    def begin(i, pieces=range(PIECES)):
        for piece in pieces:
            part = pl.ds(piece * span, span)
            passed[i, part] = partial[i, final, part].astype(passed.dtype)
            carry_copy(i, piece).start()

    def advance(i, piece, last):
        part = pl.ds(piece * span, span)
        carry_copy(i, piece).wait_recv()
        if not last:
            value = partial[i, final, part] + growth[final] * carry[i, part].astype(jnp.float32)
            passed[i, part] = value.astype(passed.dtype)
            carry_copy(i, piece).start()

    def sent(group):
        part = (pl.ds(0, 1), pl.ds(1, strip - 1), pl.ds(strip, 1))[group]
        pltpu.make_async_remote_copy(
            src_ref=passed.at[part],
            dst_ref=carry.at[part],
            send_sem=carry_send.at[(0, 1, 2)[group]],
            recv_sem=carry_recv.at[0, 0],
            device_id={"tm": moment + 1},
            device_id_type=MESH,
        ).wait_send()

    def stretch(i, carried):
        if carried:
            arrived = (relayed[...] if i == ghost[1] else carry[i]).astype(jnp.float32)
        for frame in range(frames):
            state = partial[i, frame]
            if carried:
                state = state + growth[frame] * arrived
            wide_states[i, frame] = spread(state)

    def product(sources, i):
        taps = [source - i + 1 for source in sources]
        return times([wide_states[source] for source in sources], wout, taps)

    def update(base, x):
        half = 0.5 * x
        angle = x * (ROOT + CUBIC * (x * x))
        return (base.astype(jnp.float32) + (half + half * jnp.tanh(angle))).astype(jnp.bfloat16)

    def write(i, value):
        for frame in range(frames):
            out[frame, place(i, strip)] = update(lat[frame, i], value[frame])

    cut = width // 2

    def stretch_half(i, half):
        low, count = (0, cut + span) if half == 0 else (cut - span, cut + span)
        part = pl.ds(low, count)
        keep = slice(0, cut) if half == 0 else slice(span, span + cut)
        place_of = lax.broadcasted_iota(jnp.int32, (count, channels), 0)
        arrived = carry[i, part].astype(jnp.float32)
        for frame in range(frames):
            full = partial[i, frame, part] + growth[frame] * arrived
            before, after = pltpu.roll(full, 1, 0), pltpu.roll(full, count - 1, 0)
            if half == 0:
                before = jnp.where(place_of == 0, 0.0, before)
            else:
                after = jnp.where(place_of == count - 1, 0.0, after)
            whole = jnp.concatenate([v.astype(jnp.bfloat16) for v in (before, full, after)], axis=-1)
            wide_states[i, frame, pl.ds(half * cut, cut)] = whole[keep]

    def half_times(i, half, tap):
        window = wide_states[i, :, pl.ds(half * cut, cut)].reshape(frames * cut, 3 * channels)
        value = jnp.dot(window, wout[tap], preferred_element_type=jnp.float32)
        return value.reshape(frames, cut, channels)

    def write_half(i, half, value):
        part = pl.ds(half * cut, cut)
        for frame in range(frames):
            out[frame, place(i, strip), part] = update(lat[frame, i, part], value[frame])

    def reach(side):
        return times([wide_states[ghost[side]]], wout, [2 * side])

    def wait_wout():
        pltpu.make_async_copy(wout_hbm, wout, wout_sem).wait()

    middle = list(range(1, bottom))
    first, late = middle[0], middle[1:]
    rows = pl.ds(0, 3)
    pltpu.make_async_copy(lat_hbm.at[:, rows], lat.at[:, rows], lat_sem.at[0]).wait()
    for i in range(3):
        prepare(i)
    load_table.wait()
    load_index.wait()
    chosen = index_ref[...]
    decays = jnp.zeros(chosen.shape, jnp.float32)
    for level in range(table_ref.shape[0]):
        decays = jnp.where(chosen == level, table_ref[level], decays)
    growth = [decays]
    for _ in range(frames - 1):
        growth.append(growth[-1] * decays)
    load_win(0).wait()

    @block
    def _():
        partial[first] = times([wide[0]], win, [0])

    load_win(1).wait()
    load_win(2).wait()

    @block
    def _():
        value = times([wide[1]], win, [1]) + times([wide[2]], win, [2])
        states = scan(partial[first] + value)
        for frame in range(frames):
            partial[first, frame] = states[frame]

    rows = pl.ds(3, strip - 3)
    pltpu.make_async_copy(lat_hbm.at[:, rows], lat.at[:, rows], lat_sem.at[1]).wait()
    for i in range(3, strip):
        prepare(i)

    pl.semaphore_wait(barrier, total)

    leads = jnp.logical_and(jnp.logical_not(has_before), odd == 1)

    @pl.when(leads)
    def _():
        if positions > 1:
            begin(first)
        for i in late:
            drive(i)
            if positions > 1:
                begin(i)

    @block
    def _():
        offer(0)
        drive(0)

    send(0)

    @pl.when(jnp.logical_and(jnp.logical_not(has_before), odd == 0))
    def _():
        if positions > 1:
            begin(first)

    for tap in range(3):
        load_wout(tap).start()

    @pl.when(jnp.logical_not(leads))
    def _():
        for i in late:
            drive(i)
        offer(1)
        drive(bottom)

    @pl.when(leads)
    def _():
        offer(1)
        drive(bottom)

    send(1)

    def start():
        def far():
            absorb(0, 0)
            if positions > 1:
                begin(0)
            absorb(0, 1)
            if positions > 1:
                begin(ghost[0])

        def lead():
            if positions > 1:
                for i in late:
                    begin(i)

            @guard(1)
            def _():
                absorb(1, 0)

            if positions > 1:
                begin(bottom)

            def pass_turn():
                @guard(1)
                def _():
                    pl.semaphore_signal(turn, inc=1, device_id={"rows": near[1]}, device_id_type=MESH)

            @pl.when(has[0])
            def _():
                far()
                if positions > 1:
                    sent(1)
                    sent(0)
                    pass_turn()
                    sent(2)

            @pl.when(jnp.logical_not(has[0]))
            def _():
                if positions > 1:
                    begin(0)
                    sent(1)
                    pass_turn()
                    sent(0)

        def second():
            absorb(1, 0)
            if positions > 1:
                begin(bottom)
                pl.semaphore_wait(turn, 1)

            @pl.when(has[0])
            def _():
                far()

            if positions > 1:

                @pl.when(jnp.logical_not(has[0]))
                def _():
                    begin(0)

        @pl.when(odd == 0)
        def _():
            lead()

        @pl.when(odd == 1)
        def _():
            second()

        @guard(1)
        def _():
            absorb(1, 1)
            absorb_rest(1)

        wait_wout()

        @block
        def _():
            for i in range(1, strip):
                stretch(i, False)
            for i in range(2, bottom):
                write(i, product([i - 1, i, i + 1], i))
            if paired:
                stretch(ghost[1], False)
                write(bottom, product([bottom - 1, bottom], bottom) + reach(1))
            else:
                mixed[bottom] = product([bottom - 1, bottom], bottom)

        if not paired:

            @pl.when(has[1])
            def _():
                stretch(ghost[1], False)
                mixed[bottom] = mixed[bottom] + reach(1)

            write(bottom, mixed[bottom])

        @pl.when(has[0])
        def _():
            absorb_rest(0)

        @block
        def _():
            stretch(0, False)
            write(1, product([0, 1, 2], 1))
            mixed[0] = product([0, 1], 0)

        @pl.when(has[0])
        def _():
            stretch(ghost[0], False)
            mixed[0] = mixed[0] + reach(0)

        write(0, mixed[0])

    def follow(last):
        def receive(i, pieces=range(PIECES)):
            for piece in pieces:
                advance(i, piece, last)

        def receive_ghost():
            @pl.when(has[0])
            def _():
                absorb(0, 1)
                receive(ghost[0])

        def first_rows():
            stretch(first, True)
            for i in range(first + 2):
                mixed[i] = product([first], i)

        def late_rows():
            for i in late:
                stretch(i, True)
                mixed[i + 1] = product([i], i + 1)
                mixed[i - 1] = mixed[i - 1] + product([i], i - 1)
                mixed[i] = mixed[i] + product([i], i)

        def bottom_rows(done=False):
            stretch(bottom, True)
            mixed[bottom] = mixed[bottom] + product([bottom], bottom)
            mixed[bottom - 1] = mixed[bottom - 1] + product([bottom], bottom - 1)
            for i in range(2, bottom):
                write(i, mixed[i])
            if done:
                write(bottom, mixed[bottom])

        def far_rest():
            @pl.when(has[0])
            def _():
                absorb_rest(0)

        def top_rows():
            stretch(0, True)
            mixed[0] = mixed[0] + product([0], 0)
            write(1, mixed[1] + product([0], 1))

        def core_rows():
            @guard(1)
            def _():
                relay_copy().wait_recv()

                @block
                def _():
                    stretch(ghost[1], True)
                    mixed[bottom] = mixed[bottom] + reach(1)

        waits = jnp.logical_and(has[0], odd == 1)

        def core_close():
            if paired:
                relay_copy().wait_recv()
                stretch(ghost[1], True)
                write(bottom, mixed[bottom] + reach(1))
            else:
                core_rows()
                write(bottom, mixed[bottom])

        def ghost_rows():
            @pl.when(has[0])
            def _():
                stretch(ghost[0], True)
                write(0, mixed[0] + reach(0))

            @pl.when(jnp.logical_not(has[0]))
            def _():
                write(0, mixed[0])

        def early(act):
            (block if last else pl.when(odd == 1))(act)

        def later(act):
            if not last:
                pl.when(odd == 0)(act)

        wait_wout()
        receive(first)
        if last:
            block(first_rows)
        for i in late:
            receive(i)
        if not last:
            early(first_rows)
        early(late_rows)

        @guard(1)
        def _():
            absorb(1, 0)
            absorb(1, 1)
            absorb_rest(1)

        receive(bottom)

        @guard(1)
        def _():
            relay_copy().start()

        if last:

            block(bottom_rows)

            pl.when(jnp.logical_not(waits))(core_close)

        early_pieces, last_piece = range(PIECES - 1), [PIECES - 1]

        def top_half(half):
            part = pl.ds(half * cut, cut)
            stretch_half(0, half)
            one = mixed[1, :, part] + half_times(0, half, 0)
            two = mixed[0, :, part] + half_times(0, half, 1)
            write_half(1, half, one)
            write_half(0, half, two)

        def free_end():
            receive(0, early_pieces)
            top_half(0)
            receive(0, last_piece)
            top_half(1)

        def far_end():
            absorb(0, 0)
            receive(0)
            absorb_rest(0)
            block(top_rows)

            pl.when(odd == 1)(core_close)
            absorb(0, 1)
            receive(ghost[0])

            @block
            def _():
                stretch(ghost[0], True)
                write(0, mixed[0] + reach(0))

        if last:
            pl.when(jnp.logical_not(has[0]))(free_end)
            pl.when(has[0])(far_end)
        else:

            @pl.when(has[0])
            def _():
                absorb(0, 0)

            receive(0)
            receive_ghost()
            later(first_rows)
            later(late_rows)
            core_rows()
            block(lambda: bottom_rows(True))
            far_rest()
            block(top_rows)
            ghost_rows()

    @pl.when(jnp.logical_not(has_before))
    def _():
        start()

    @pl.when(jnp.logical_and(has_before, has_after))
    def _():
        follow(False)

    @pl.when(jnp.logical_and(has_before, jnp.logical_not(has_after)))
    def _():
        follow(True)

    for side in range(2):

        @pl.when(has[side])
        def _():
            share_sent(side)

    @pl.when(jnp.logical_and(has[1], has_before))
    def _():
        relay_copy().wait_send()

    pending = jnp.logical_and(has_after, jnp.logical_or(has_before, odd == 1))

    @pl.when(pending)
    def _():
        sent(1)
        sent(0)

    @pl.when(jnp.logical_and(has[0], pending))
    def _():
        sent(2)


def local(positions, strips, latents, weight_in, weight_out, decay_table, decay_index):
    frames, strip, width, channels = latents.shape
    link = jnp.bfloat16 if positions <= 8 else jnp.float32
    half = jnp.bfloat16
    dma = pltpu.SemaphoreType.DMA
    anywhere = pl.BlockSpec(memory_space=pl.ANY)
    return pl.pallas_call(
        functools.partial(kernel, positions, strips),
        out_shape=jax.ShapeDtypeStruct(latents.shape, latents.dtype),
        in_specs=[anywhere] * 5,
        out_specs=pl.BlockSpec(memory_space=pltpu.VMEM),
        scratch_shapes=[
            pltpu.VMEM((frames, strip, width, channels), half),
            pltpu.VMEM((9 * channels, channels), half),
            pltpu.VMEM((3, 3 * channels, channels), half),
            pltpu.VMEM((strip, frames, width, 3 * channels), half),
            pltpu.VMEM((strip + 2, frames, width, channels), jnp.float32),
            pltpu.VMEM((2, frames, 2, width, channels), half),
            pltpu.VMEM((2, frames, 2, width, channels), half),
            pltpu.VMEM((strip + 1, width, channels), link),
            pltpu.VMEM((strip + 1, width, channels), link),
            pltpu.VMEM((width, channels), link),
            pltpu.VMEM((strip, frames, width, channels), jnp.float32),
            pltpu.SMEM(decay_table.shape, jnp.float32),
            pltpu.VMEM((1, channels), jnp.int32),
            pltpu.VMEM((strip + 2, frames, width, 3 * channels), half),
            dma((2,)),
            dma((3,)),
            dma,
            dma((2,)),
            dma((2,)),
            dma((2, 3)),
            dma((3,)),
            dma((strip + 1, PIECES)),
            dma,
            dma,
            pltpu.SemaphoreType.REGULAR,
        ],
        compiler_params=pltpu.CompilerParams(collective_id=0, has_side_effects=True, vmem_limit_bytes=32 * 1024 * 1024),
    )(
        pltpu.with_memory_space_constraint(latents, pltpu.HBM),
        pltpu.with_memory_space_constraint(weight_in.reshape(3, 3 * channels, channels), pltpu.HBM),
        pltpu.with_memory_space_constraint(weight_out.reshape(3, 3 * channels, channels), pltpu.HBM),
        pltpu.with_memory_space_constraint(decay_table, pltpu.HBM),
        pltpu.with_memory_space_constraint(decay_index.reshape(1, channels), pltpu.HBM),
    )


def solution(mesh):
    in_specs = (P(("groups", "tm"), "rows", None, None), P(), P(), P(), P())
    out_specs = P(("groups", "tm"), "rows", None, None)
    body = functools.partial(local, mesh.shape["tm"], mesh.shape["rows"])
    return jax.shard_map(body, mesh=mesh, in_specs=in_specs, out_specs=out_specs, check_vma=False)
```

```python
import functools
import math

import jax
import jax.numpy as jnp
from jax import lax
from jax.experimental import pallas as pl
from jax.experimental.pallas import tpu as pltpu
from jax.sharding import PartitionSpec as P

MESH = pl.DeviceIdType.MESH
PIECES = 4
ROOT = (2.0 / math.pi) ** 0.5
CUBIC = 0.044715 * ROOT


def update(base, x):
    half = 0.5 * x
    angle = x * (ROOT + CUBIC * (x * x))
    return (base.astype(jnp.float32) + (half + half * jnp.tanh(angle))).astype(jnp.bfloat16)


def kernel(
    positions,
    strips,
    lat_hbm,
    win_hbm,
    wout_hbm,
    table_hbm,
    index_hbm,
    out,
    kept,
    open_row,
    lat,
    win,
    wout,
    wide,
    partial,
    share,
    shared,
    carry,
    passed,
    relayed,
    mixed,
    table_ref,
    index_ref,
    wide_states,
    lat_sem,
    win_sem,
    wout_sem,
    small_sem,
    share_send,
    share_recv,
    carry_send,
    carry_recv,
    relay_send,
    relay_recv,
    turn,
):
    frames, strip, width, channels = lat.shape
    row = lax.axis_index("rows")
    moment = lax.axis_index("tm")
    odd = lax.rem(row, 2)
    span = width // PIECES
    bottom = strip - 1
    final = frames - 1
    edge = (0, bottom)
    ghost = (strip, strip + 1)
    near = (row - 1 + 2 * odd, row + 1 - 2 * odd)
    has = tuple(jnp.logical_and(at >= 0, at < strips) for at in near)
    paired = strips % 2 == 0
    depth = 3 * channels
    has_before, has_after = moment > 0, moment < positions - 1

    def guard(side):
        if side == 1 and paired:
            return lambda act: act()
        return pl.when(has[side])

    def place(i, count):
        return i + odd * (count - 1 - 2 * i)

    def load_lat(i):
        return pltpu.make_async_copy(lat_hbm.at[:, place(i, strip)], lat.at[:, i], lat_sem.at[0 if i < 3 else 1])

    def load_win(tap):
        return pltpu.make_async_copy(win_hbm.at[place(tap, 3)], win.at[pl.ds(tap * depth, depth)], win_sem.at[tap])

    def load_wout(tap):
        return pltpu.make_async_copy(wout_hbm.at[place(tap, 3)], wout.at[tap], wout_sem)

    load_table = pltpu.make_async_copy(table_hbm, table_ref, small_sem.at[0])
    load_index = pltpu.make_async_copy(index_hbm, index_ref, small_sem.at[1])

    for i in range(3):
        load_lat(i).start()
    load_win(0).start()

    barrier = pltpu.get_barrier_semaphore()
    greeted = (
        (has[0], {"rows": near[0]}),
        (has[1], {"rows": near[1]}),
        (has_before, {"tm": moment - 1}),
        (has_after, {"tm": moment + 1}),
    )
    total = 0
    for exists, where in greeted:
        total = total + exists.astype(jnp.int32)

        @pl.when(exists)
        def _():
            pl.semaphore_signal(barrier, inc=1, device_id=where, device_id_type=MESH)

    load_table.start()
    load_index.start()
    for tap in range(1, 3):
        load_win(tap).start()
    for i in range(3, strip):
        load_lat(i).start()

    def share_copy(side, kind, frame):
        return pltpu.make_async_remote_copy(
            src_ref=share.at[side, frame, kind],
            dst_ref=shared.at[side, frame, kind],
            send_sem=share_send.at[side],
            recv_sem=share_recv.at[side, kind if frame == final else 2],
            device_id={"rows": near[side]},
            device_id_type=MESH,
        )

    def relay_copy():
        return pltpu.make_async_remote_copy(
            src_ref=carry.at[bottom],
            dst_ref=relayed,
            send_sem=relay_send,
            recv_sem=relay_recv,
            device_id={"rows": near[1]},
            device_id_type=MESH,
        )

    def carry_copy(i, piece):
        part = pl.ds(piece * span, span)
        return pltpu.make_async_remote_copy(
            src_ref=passed.at[i, part],
            dst_ref=carry.at[i, part],
            send_sem=carry_send.at[min(i, 1) if i < strip else 2],
            recv_sem=carry_recv.at[i, piece],
            device_id={"tm": moment + 1},
            device_id_type=MESH,
        )

    column = lax.broadcasted_iota(jnp.int32, (width, channels), 0)

    def spread(value):
        full = value.astype(jnp.float32)
        before = jnp.where(column == 0, 0.0, pltpu.roll(full, 1, 0))
        after = jnp.where(column == width - 1, 0.0, pltpu.roll(full, width - 1, 0))
        middle = value.astype(jnp.bfloat16)
        return jnp.concatenate([before.astype(jnp.bfloat16), middle, after.astype(jnp.bfloat16)], axis=-1)

    def prepare(i):
        for frame in range(frames):
            wide[i, frame] = spread(lat[frame, i])

    def times(rows, weights, taps):
        window = [r.reshape(frames * width, 3 * channels) for r in rows]
        window = window[0] if len(rows) == 1 else jnp.concatenate(window, axis=-1)
        if len(weights.shape) == 3:
            factor = weights[taps[0] : taps[-1] + 1].reshape(len(taps) * depth, channels)
        else:
            factor = weights[taps[0] * depth : (taps[-1] + 1) * depth]
        value = jnp.dot(window, factor, preferred_element_type=jnp.float32)
        return value.reshape(frames, width, channels)

    def scan(value):
        running = [value[0]]
        for frame in range(1, frames):
            running.append(decays * running[-1] + value[frame])
        return running

    def drive(i):
        taps = [tap for tap in range(3) if 0 <= i + tap - 1 < strip]
        states = scan(times([wide[i + tap - 1] for tap in taps], win, taps))
        for frame in range(frames):
            partial[i, frame] = states[frame]
            if i in edge:
                share[edge.index(i), frame, 1] = states[frame].astype(jnp.bfloat16)

    def offer(side):
        states = scan(times([wide[edge[side]]], win, [2 - 2 * side]))
        for frame in range(frames):
            partial[ghost[side], frame] = states[frame]
            share[side, frame, 0] = states[frame].astype(jnp.bfloat16)

    def send(side):
        @guard(side)
        def _():
            for frame in reversed(range(frames)):
                for kind in range(2):
                    share_copy(side, kind, frame).start()

    def add_share(side, kind, frame):
        i = (edge, ghost)[kind][side]
        partial[i, frame] = partial[i, frame] + shared[side, frame, kind].astype(jnp.float32)

    def absorb(side, kind):
        share_copy(side, kind, final).wait_recv()
        add_share(side, kind, final)

    def absorb_rest(side):
        if final == 0:
            return
        part = pl.ds(0, final)
        pltpu.make_async_remote_copy(
            src_ref=share.at[side, part],
            dst_ref=shared.at[side, part],
            send_sem=share_send.at[side],
            recv_sem=share_recv.at[side, 2],
            device_id={"rows": near[side]},
            device_id_type=MESH,
        ).wait_recv()
        for frame in range(final):
            for kind in range(2):
                add_share(side, kind, frame)

    def share_sent(side):
        pltpu.make_async_remote_copy(
            src_ref=share.at[side],
            dst_ref=shared.at[side],
            send_sem=share_send.at[side],
            recv_sem=share_recv.at[side, 2],
            device_id={"rows": near[side]},
            device_id_type=MESH,
        ).wait_send()

    def block(act):
        pl.when(row >= 0)(act)

    def begin(i, pieces=range(PIECES)):
        for piece in pieces:
            part = pl.ds(piece * span, span)
            passed[i, part] = partial[i, final, part].astype(passed.dtype)
            carry_copy(i, piece).start()

    def advance(i, piece, last):
        part = pl.ds(piece * span, span)
        carry_copy(i, piece).wait_recv()
        if not last:
            value = partial[i, final, part] + growth[final] * carry[i, part].astype(jnp.float32)
            passed[i, part] = value.astype(passed.dtype)
            carry_copy(i, piece).start()

    def sent(group):
        part = (pl.ds(0, 1), pl.ds(1, strip - 1), pl.ds(strip, 1))[group]
        pltpu.make_async_remote_copy(
            src_ref=passed.at[part],
            dst_ref=carry.at[part],
            send_sem=carry_send.at[(0, 1, 2)[group]],
            recv_sem=carry_recv.at[0, 0],
            device_id={"tm": moment + 1},
            device_id_type=MESH,
        ).wait_send()

    def stretch(i, carried):
        if carried:
            arrived = (relayed[...] if i == ghost[1] else carry[i]).astype(jnp.float32)
        for frame in range(frames):
            state = partial[i, frame]
            if carried:
                state = state + growth[frame] * arrived
            wide_states[i, frame] = spread(state)

    def product(sources, i):
        taps = [source - i + 1 for source in sources]
        return times([wide_states[source] for source in sources], wout, taps)

    def write(i, value):
        for frame in range(frames):
            if i == 0:
                open_row[frame] = value[frame]
                continue
            out[frame, place(i, strip)] = update(lat[frame, i], value[frame])

    cut = width // 2

    def stretch_half(i, half):
        low, count = (0, cut + span) if half == 0 else (cut - span, cut + span)
        part = pl.ds(low, count)
        keep = slice(0, cut) if half == 0 else slice(span, span + cut)
        place_of = lax.broadcasted_iota(jnp.int32, (count, channels), 0)
        arrived = carry[i, part].astype(jnp.float32)
        for frame in range(frames):
            full = partial[i, frame, part] + growth[frame] * arrived
            before, after = pltpu.roll(full, 1, 0), pltpu.roll(full, count - 1, 0)
            if half == 0:
                before = jnp.where(place_of == 0, 0.0, before)
            else:
                after = jnp.where(place_of == count - 1, 0.0, after)
            whole = jnp.concatenate([v.astype(jnp.bfloat16) for v in (before, full, after)], axis=-1)
            wide_states[i, frame, pl.ds(half * cut, cut)] = whole[keep]

    def half_times(i, half, tap):
        window = wide_states[i, :, pl.ds(half * cut, cut)].reshape(frames * cut, 3 * channels)
        value = jnp.dot(window, wout[tap], preferred_element_type=jnp.float32)
        return value.reshape(frames, cut, channels)

    def write_half(i, half, value):
        part = pl.ds(half * cut, cut)
        for frame in range(frames):
            if i == 0:
                open_row[frame, part] = value[frame]
                continue
            out[frame, place(i, strip), part] = update(lat[frame, i, part], value[frame])

    def reach(side):
        return times([wide_states[ghost[side]]], wout, [2 * side])

    def wait_wout():
        pltpu.make_async_copy(wout_hbm, wout, wout_sem).wait()

    middle = list(range(1, bottom))
    first, late = middle[0], middle[1:]
    rows = pl.ds(0, 3)
    pltpu.make_async_copy(lat_hbm.at[:, rows], lat.at[:, rows], lat_sem.at[0]).wait()
    for i in range(3):
        prepare(i)
    load_table.wait()
    load_index.wait()
    chosen = index_ref[...]
    decays = jnp.zeros(chosen.shape, jnp.float32)
    for level in range(table_ref.shape[0]):
        decays = jnp.where(chosen == level, table_ref[level], decays)
    growth = [decays]
    for _ in range(frames - 1):
        growth.append(growth[-1] * decays)
    load_win(0).wait()

    @block
    def _():
        partial[first] = times([wide[0]], win, [0])

    load_win(1).wait()
    load_win(2).wait()

    @block
    def _():
        value = times([wide[1]], win, [1]) + times([wide[2]], win, [2])
        states = scan(partial[first] + value)
        for frame in range(frames):
            partial[first, frame] = states[frame]

    rows = pl.ds(3, strip - 3)
    pltpu.make_async_copy(lat_hbm.at[:, rows], lat.at[:, rows], lat_sem.at[1]).wait()
    for i in range(3, strip):
        prepare(i)

    kept[...] = lat[:, 0]
    pl.semaphore_wait(barrier, total)

    leads = jnp.logical_and(jnp.logical_not(has_before), odd == 1)

    @pl.when(leads)
    def _():
        if positions > 1:
            begin(first)
        for i in late:
            drive(i)
            if positions > 1:
                begin(i)

    @block
    def _():
        offer(0)
        drive(0)

    send(0)

    @pl.when(jnp.logical_and(jnp.logical_not(has_before), odd == 0))
    def _():
        if positions > 1:
            begin(first)

    for tap in range(3):
        load_wout(tap).start()

    @pl.when(jnp.logical_not(leads))
    def _():
        for i in late:
            drive(i)
        offer(1)
        drive(bottom)

    @pl.when(leads)
    def _():
        offer(1)
        drive(bottom)

    send(1)

    def start():
        def far():
            absorb(0, 0)
            if positions > 1:
                begin(0)
            absorb(0, 1)
            if positions > 1:
                begin(ghost[0])

        def lead():
            if positions > 1:
                for i in late:
                    begin(i)

            @guard(1)
            def _():
                absorb(1, 0)

            if positions > 1:
                begin(bottom)

            def pass_turn():
                @guard(1)
                def _():
                    pl.semaphore_signal(turn, inc=1, device_id={"rows": near[1]}, device_id_type=MESH)

            @pl.when(has[0])
            def _():
                far()
                if positions > 1:
                    sent(1)
                    sent(0)
                    pass_turn()
                    sent(2)

            @pl.when(jnp.logical_not(has[0]))
            def _():
                if positions > 1:
                    begin(0)
                    sent(1)
                    pass_turn()
                    sent(0)

        def second():
            absorb(1, 0)
            if positions > 1:
                begin(bottom)
                pl.semaphore_wait(turn, 1)

            @pl.when(has[0])
            def _():
                far()

            if positions > 1:

                @pl.when(jnp.logical_not(has[0]))
                def _():
                    begin(0)

        @pl.when(odd == 0)
        def _():
            lead()

        @pl.when(odd == 1)
        def _():
            second()

        @guard(1)
        def _():
            absorb(1, 1)
            absorb_rest(1)

        wait_wout()

        @block
        def _():
            for i in range(1, strip):
                stretch(i, False)
            for i in range(2, bottom):
                write(i, product([i - 1, i, i + 1], i))
            if paired:
                stretch(ghost[1], False)
                write(bottom, product([bottom - 1, bottom], bottom) + reach(1))
            else:
                mixed[bottom] = product([bottom - 1, bottom], bottom)

        if not paired:

            @pl.when(has[1])
            def _():
                stretch(ghost[1], False)
                mixed[bottom] = mixed[bottom] + reach(1)

            write(bottom, mixed[bottom])

        @pl.when(has[0])
        def _():
            absorb_rest(0)

        @block
        def _():
            stretch(0, False)
            write(1, product([0, 1, 2], 1))
            mixed[0] = product([0, 1], 0)

        @pl.when(has[0])
        def _():
            stretch(ghost[0], False)
            mixed[0] = mixed[0] + reach(0)

        write(0, mixed[0])

    def follow(last):
        def receive(i, pieces=range(PIECES)):
            for piece in pieces:
                advance(i, piece, last)

        def receive_ghost():
            @pl.when(has[0])
            def _():
                absorb(0, 1)
                receive(ghost[0])

        def first_rows():
            stretch(first, True)
            for i in range(first + 2):
                mixed[i] = product([first], i)

        def late_rows():
            for i in late:
                stretch(i, True)
                mixed[i + 1] = product([i], i + 1)
                mixed[i - 1] = mixed[i - 1] + product([i], i - 1)
                mixed[i] = mixed[i] + product([i], i)

        def bottom_rows(done=False):
            stretch(bottom, True)
            mixed[bottom] = mixed[bottom] + product([bottom], bottom)
            mixed[bottom - 1] = mixed[bottom - 1] + product([bottom], bottom - 1)
            for i in range(2, bottom):
                write(i, mixed[i])
            if done:
                write(bottom, mixed[bottom])

        def far_rest():
            @pl.when(has[0])
            def _():
                absorb_rest(0)

        def top_rows():
            stretch(0, True)
            mixed[0] = mixed[0] + product([0], 0)
            write(1, mixed[1] + product([0], 1))

        def core_rows():
            @guard(1)
            def _():
                relay_copy().wait_recv()

                @block
                def _():
                    stretch(ghost[1], True)
                    mixed[bottom] = mixed[bottom] + reach(1)

        waits = jnp.logical_and(has[0], odd == 1)

        def core_close():
            if paired:
                relay_copy().wait_recv()
                stretch(ghost[1], True)
                write(bottom, mixed[bottom] + reach(1))
            else:
                core_rows()
                write(bottom, mixed[bottom])

        def ghost_rows():
            @pl.when(has[0])
            def _():
                stretch(ghost[0], True)
                write(0, mixed[0] + reach(0))

            @pl.when(jnp.logical_not(has[0]))
            def _():
                write(0, mixed[0])

        def early(act):
            (block if last else pl.when(odd == 1))(act)

        def later(act):
            if not last:
                pl.when(odd == 0)(act)

        wait_wout()
        receive(first)
        if last:
            block(first_rows)
        for i in late:
            receive(i)
        if not last:
            early(first_rows)
        early(late_rows)

        @guard(1)
        def _():
            absorb(1, 0)
            absorb(1, 1)
            absorb_rest(1)

        receive(bottom)

        @guard(1)
        def _():
            relay_copy().start()

        if last:

            block(bottom_rows)

            pl.when(jnp.logical_not(waits))(core_close)

        early_pieces, last_piece = range(PIECES - 1), [PIECES - 1]

        def top_half(half):
            part = pl.ds(half * cut, cut)
            stretch_half(0, half)
            one = mixed[1, :, part] + half_times(0, half, 0)
            two = mixed[0, :, part] + half_times(0, half, 1)
            write_half(1, half, one)
            write_half(0, half, two)

        def free_end():
            receive(0, early_pieces)
            top_half(0)
            receive(0, last_piece)
            top_half(1)

        def far_end():
            absorb(0, 0)
            receive(0)
            absorb_rest(0)
            block(top_rows)

            pl.when(odd == 1)(core_close)
            absorb(0, 1)
            receive(ghost[0])

            @block
            def _():
                stretch(ghost[0], True)
                write(0, mixed[0] + reach(0))

        if last:
            pl.when(jnp.logical_not(has[0]))(free_end)
            pl.when(has[0])(far_end)
        else:

            @pl.when(has[0])
            def _():
                absorb(0, 0)

            receive(0)
            receive_ghost()
            later(first_rows)
            later(late_rows)
            core_rows()
            block(lambda: bottom_rows(True))
            far_rest()
            block(top_rows)
            ghost_rows()

    @pl.when(jnp.logical_not(has_before))
    def _():
        start()

    @pl.when(jnp.logical_and(has_before, has_after))
    def _():
        follow(False)

    @pl.when(jnp.logical_and(has_before, jnp.logical_not(has_after)))
    def _():
        follow(True)

    for side in range(2):

        @pl.when(has[side])
        def _():
            share_sent(side)

    @pl.when(jnp.logical_and(has[1], has_before))
    def _():
        relay_copy().wait_send()

    pending = jnp.logical_and(has_after, jnp.logical_or(has_before, odd == 1))

    @pl.when(pending)
    def _():
        sent(1)
        sent(0)

    @pl.when(jnp.logical_and(has[0], pending))
    def _():
        sent(2)


def local(positions, strips, latents, weight_in, weight_out, decay_table, decay_index):
    frames, strip, width, channels = latents.shape
    link = jnp.bfloat16 if positions <= 8 else jnp.float32
    half = jnp.bfloat16
    dma = pltpu.SemaphoreType.DMA
    anywhere = pl.BlockSpec(memory_space=pl.ANY)
    done = pl.pallas_call(
        functools.partial(kernel, positions, strips),
        out_shape=[
            jax.ShapeDtypeStruct(latents.shape, latents.dtype),
            jax.ShapeDtypeStruct((frames, width, channels), latents.dtype),
            jax.ShapeDtypeStruct((frames, width, channels), jnp.float32),
        ],
        in_specs=[anywhere] * 5,
        out_specs=[pl.BlockSpec(memory_space=pltpu.VMEM)] * 3,
        scratch_shapes=[
            pltpu.VMEM((frames, strip, width, channels), half),
            pltpu.VMEM((9 * channels, channels), half),
            pltpu.VMEM((3, 3 * channels, channels), half),
            pltpu.VMEM((strip, frames, width, 3 * channels), half),
            pltpu.VMEM((strip + 2, frames, width, channels), jnp.float32),
            pltpu.VMEM((2, frames, 2, width, channels), half),
            pltpu.VMEM((2, frames, 2, width, channels), half),
            pltpu.VMEM((strip + 1, width, channels), link),
            pltpu.VMEM((strip + 1, width, channels), link),
            pltpu.VMEM((width, channels), link),
            pltpu.VMEM((strip, frames, width, channels), jnp.float32),
            pltpu.SMEM(decay_table.shape, jnp.float32),
            pltpu.VMEM((1, channels), jnp.int32),
            pltpu.VMEM((strip + 2, frames, width, 3 * channels), half),
            dma((2,)),
            dma((3,)),
            dma,
            dma((2,)),
            dma((2,)),
            dma((2, 3)),
            dma((3,)),
            dma((strip + 1, PIECES)),
            dma,
            dma,
            pltpu.SemaphoreType.REGULAR,
        ],
        compiler_params=pltpu.CompilerParams(collective_id=0, has_side_effects=True, vmem_limit_bytes=32 * 1024 * 1024),
    )(
        pltpu.with_memory_space_constraint(latents, pltpu.HBM),
        pltpu.with_memory_space_constraint(weight_in.reshape(3, 3 * channels, channels), pltpu.HBM),
        pltpu.with_memory_space_constraint(weight_out.reshape(3, 3 * channels, channels), pltpu.HBM),
        pltpu.with_memory_space_constraint(decay_table, pltpu.HBM),
        pltpu.with_memory_space_constraint(decay_index.reshape(1, channels), pltpu.HBM),
    )
    return pl.pallas_call(
        hand_out,
        out_shape=jax.ShapeDtypeStruct(latents.shape, latents.dtype),
        in_specs=[pl.BlockSpec(memory_space=pl.ANY)] + [pl.BlockSpec(memory_space=pltpu.VMEM)] * 2,
        out_specs=pl.BlockSpec(memory_space=pltpu.HBM),
        scratch_shapes=[pltpu.VMEM((frames, width, channels), half), dma((2,))],
    )(*[pltpu.with_memory_space_constraint(value, pltpu.VMEM) for value in done])


def hand_out(source, kept, open_row, target, row_out, sem):
    frames, strip = source.shape[:2]
    odd = lax.rem(lax.axis_index("rows"), 2)
    rest = pl.ds(1 - odd, strip - 1)
    first = pltpu.make_async_copy(source.at[:, rest], target.at[:, rest], sem.at[0])
    second = pltpu.make_async_copy(row_out, target.at[:, odd * (strip - 1)], sem.at[1])
    first.start()
    for frame in range(frames):
        row_out[frame] = update(kept[frame], open_row[frame])
    second.start()
    first.wait()
    second.wait()


def solution(mesh):
    in_specs = (P(("groups", "tm"), "rows", None, None), P(), P(), P(), P())
    out_specs = P(("groups", "tm"), "rows", None, None)
    body = functools.partial(local, mesh.shape["tm"], mesh.shape["rows"])
    return jax.shard_map(body, mesh=mesh, in_specs=in_specs, out_specs=out_specs, check_vma=False)
```

```python
import functools
import math

import jax
import jax.numpy as jnp
from jax import lax
from jax.experimental import pallas as pl
from jax.experimental.pallas import tpu as pltpu
from jax.sharding import PartitionSpec as P

MESH = pl.DeviceIdType.MESH
PIECES = 4
ROOT = (2.0 / math.pi) ** 0.5
CUBIC = 0.044715 * ROOT


def update(base, x):
    half = 0.5 * x
    angle = x * (ROOT + CUBIC * (x * x))
    return (base.astype(jnp.float32) + (half + half * jnp.tanh(angle))).astype(jnp.bfloat16)


def kernel(
    positions,
    strips,
    lat_hbm,
    win_hbm,
    wout_hbm,
    table_hbm,
    index_hbm,
    out,
    kept,
    open_row,
    lat,
    win,
    wout,
    wide,
    partial,
    share,
    shared,
    carry,
    passed,
    relayed,
    mixed,
    table_ref,
    index_ref,
    wide_states,
    lat_sem,
    win_sem,
    wout_sem,
    small_sem,
    share_send,
    share_recv,
    carry_send,
    carry_recv,
    relay_send,
    relay_recv,
    turn,
):
    frames, strip, width, channels = lat.shape
    row = lax.axis_index("rows")
    moment = lax.axis_index("tm")
    odd = lax.rem(row, 2)
    span = width // PIECES
    bottom = strip - 1
    final = frames - 1
    edge = (0, bottom)
    ghost = (strip, strip + 1)
    near = (row - 1 + 2 * odd, row + 1 - 2 * odd)
    has = tuple(jnp.logical_and(at >= 0, at < strips) for at in near)
    paired = strips % 2 == 0
    depth = 3 * channels
    has_before, has_after = moment > 0, moment < positions - 1

    def guard(side):
        if side == 1 and paired:
            return lambda act: act()
        return pl.when(has[side])

    def place(i, count):
        return i + odd * (count - 1 - 2 * i)

    def load_lat(i):
        return pltpu.make_async_copy(lat_hbm.at[:, place(i, strip)], lat.at[:, i], lat_sem.at[0 if i < 3 else 1])

    def load_win(tap):
        return pltpu.make_async_copy(win_hbm.at[place(tap, 3)], win.at[pl.ds(tap * depth, depth)], win_sem.at[tap])

    def load_wout(tap):
        return pltpu.make_async_copy(wout_hbm.at[place(tap, 3)], wout.at[tap], wout_sem)

    load_table = pltpu.make_async_copy(table_hbm, table_ref, small_sem.at[0])
    load_index = pltpu.make_async_copy(index_hbm, index_ref, small_sem.at[1])

    for i in range(3):
        load_lat(i).start()
    load_win(0).start()

    barrier = pltpu.get_barrier_semaphore()
    greeted = (
        (has[0], {"rows": near[0]}),
        (has[1], {"rows": near[1]}),
        (has_before, {"tm": moment - 1}),
        (has_after, {"tm": moment + 1}),
    )
    total = 0
    for exists, where in greeted:
        total = total + exists.astype(jnp.int32)

        @pl.when(exists)
        def _():
            pl.semaphore_signal(barrier, inc=1, device_id=where, device_id_type=MESH)

    load_table.start()
    load_index.start()
    for tap in range(1, 3):
        load_win(tap).start()
    for i in range(3, strip):
        load_lat(i).start()

    def share_copy(side, kind, frame):
        return pltpu.make_async_remote_copy(
            src_ref=share.at[side, frame, kind],
            dst_ref=shared.at[side, frame, kind],
            send_sem=share_send.at[side],
            recv_sem=share_recv.at[side, kind if frame == final else 2],
            device_id={"rows": near[side]},
            device_id_type=MESH,
        )

    def relay_copy():
        return pltpu.make_async_remote_copy(
            src_ref=carry.at[bottom],
            dst_ref=relayed,
            send_sem=relay_send,
            recv_sem=relay_recv,
            device_id={"rows": near[1]},
            device_id_type=MESH,
        )

    def carry_copy(i, piece):
        part = pl.ds(piece * span, span)
        return pltpu.make_async_remote_copy(
            src_ref=passed.at[i, part],
            dst_ref=carry.at[i, part],
            send_sem=carry_send.at[min(i, 1) if i < strip else 2],
            recv_sem=carry_recv.at[i, piece],
            device_id={"tm": moment + 1},
            device_id_type=MESH,
        )

    column = lax.broadcasted_iota(jnp.int32, (width, channels), 0)

    def spread(value):
        full = value.astype(jnp.float32)
        before = jnp.where(column == 0, 0.0, pltpu.roll(full, 1, 0))
        after = jnp.where(column == width - 1, 0.0, pltpu.roll(full, width - 1, 0))
        middle = value.astype(jnp.bfloat16)
        return jnp.concatenate([before.astype(jnp.bfloat16), middle, after.astype(jnp.bfloat16)], axis=-1)

    def prepare(i):
        for frame in range(frames):
            wide[i, frame] = spread(lat[frame, i])

    def times(rows, weights, taps):
        window = [r.reshape(frames * width, 3 * channels) for r in rows]
        window = window[0] if len(rows) == 1 else jnp.concatenate(window, axis=-1)
        if len(weights.shape) == 3:
            factor = weights[taps[0] : taps[-1] + 1].reshape(len(taps) * depth, channels)
        else:
            factor = weights[taps[0] * depth : (taps[-1] + 1) * depth]
        value = jnp.dot(window, factor, preferred_element_type=jnp.float32)
        return value.reshape(frames, width, channels)

    def scan(value):
        running = [value[0]]
        for frame in range(1, frames):
            running.append(decays * running[-1] + value[frame])
        return running

    def drive(i):
        taps = [tap for tap in range(3) if 0 <= i + tap - 1 < strip]
        states = scan(times([wide[i + tap - 1] for tap in taps], win, taps))
        for frame in range(frames):
            partial[i, frame] = states[frame]
            if i in edge:
                share[edge.index(i), frame, 1] = states[frame].astype(jnp.bfloat16)

    def offer(side):
        states = scan(times([wide[edge[side]]], win, [2 - 2 * side]))
        for frame in range(frames):
            partial[ghost[side], frame] = states[frame]
            share[side, frame, 0] = states[frame].astype(jnp.bfloat16)

    def send(side):
        @guard(side)
        def _():
            for frame in reversed(range(frames)):
                for kind in range(2):
                    share_copy(side, kind, frame).start()

    def add_share(side, kind, frame):
        i = (edge, ghost)[kind][side]
        partial[i, frame] = partial[i, frame] + shared[side, frame, kind].astype(jnp.float32)

    def absorb(side, kind):
        share_copy(side, kind, final).wait_recv()
        add_share(side, kind, final)

    def absorb_rest(side):
        if final == 0:
            return
        part = pl.ds(0, final)
        pltpu.make_async_remote_copy(
            src_ref=share.at[side, part],
            dst_ref=shared.at[side, part],
            send_sem=share_send.at[side],
            recv_sem=share_recv.at[side, 2],
            device_id={"rows": near[side]},
            device_id_type=MESH,
        ).wait_recv()
        for frame in range(final):
            for kind in range(2):
                add_share(side, kind, frame)

    def share_sent(side):
        pltpu.make_async_remote_copy(
            src_ref=share.at[side],
            dst_ref=shared.at[side],
            send_sem=share_send.at[side],
            recv_sem=share_recv.at[side, 2],
            device_id={"rows": near[side]},
            device_id_type=MESH,
        ).wait_send()

    def block(act):
        pl.when(row >= 0)(act)

    def begin(i, pieces=range(PIECES)):
        for piece in pieces:
            part = pl.ds(piece * span, span)
            passed[i, part] = partial[i, final, part].astype(passed.dtype)
            carry_copy(i, piece).start()

    def advance(i, piece, last):
        part = pl.ds(piece * span, span)
        carry_copy(i, piece).wait_recv()
        if not last:
            value = partial[i, final, part] + growth[final] * carry[i, part].astype(jnp.float32)
            passed[i, part] = value.astype(passed.dtype)
            carry_copy(i, piece).start()

    def sent(group):
        part = (pl.ds(0, 1), pl.ds(1, strip - 1), pl.ds(strip, 1))[group]
        pltpu.make_async_remote_copy(
            src_ref=passed.at[part],
            dst_ref=carry.at[part],
            send_sem=carry_send.at[(0, 1, 2)[group]],
            recv_sem=carry_recv.at[0, 0],
            device_id={"tm": moment + 1},
            device_id_type=MESH,
        ).wait_send()

    def stretch(i, carried):
        if carried:
            arrived = (relayed[...] if i == ghost[1] else carry[i]).astype(jnp.float32)
        for frame in range(frames):
            state = partial[i, frame]
            if carried:
                state = state + growth[frame] * arrived
            wide_states[i, frame] = spread(state)

    def product(sources, i):
        taps = [source - i + 1 for source in sources]
        return times([wide_states[source] for source in sources], wout, taps)

    def write(i, value):
        for frame in range(frames):
            if i == 0:
                open_row[frame] = value[frame]
                continue
            out[frame, place(i, strip)] = update(lat[frame, i], value[frame])

    cut = width // 2

    def stretch_half(i, half):
        low, count = (0, cut + span) if half == 0 else (cut - span, cut + span)
        part = pl.ds(low, count)
        keep = slice(0, cut) if half == 0 else slice(span, span + cut)
        place_of = lax.broadcasted_iota(jnp.int32, (count, channels), 0)
        arrived = carry[i, part].astype(jnp.float32)
        for frame in range(frames):
            full = partial[i, frame, part] + growth[frame] * arrived
            before, after = pltpu.roll(full, 1, 0), pltpu.roll(full, count - 1, 0)
            if half == 0:
                before = jnp.where(place_of == 0, 0.0, before)
            else:
                after = jnp.where(place_of == count - 1, 0.0, after)
            whole = jnp.concatenate([v.astype(jnp.bfloat16) for v in (before, full, after)], axis=-1)
            wide_states[i, frame, pl.ds(half * cut, cut)] = whole[keep]

    def half_times(i, half, tap):
        window = wide_states[i, :, pl.ds(half * cut, cut)].reshape(frames * cut, 3 * channels)
        value = jnp.dot(window, wout[tap], preferred_element_type=jnp.float32)
        return value.reshape(frames, cut, channels)

    def write_half(i, half, value):
        part = pl.ds(half * cut, cut)
        for frame in range(frames):
            if i == 0:
                open_row[frame, part] = value[frame]
                continue
            out[frame, place(i, strip), part] = update(lat[frame, i, part], value[frame])

    def reach(side):
        return times([wide_states[ghost[side]]], wout, [2 * side])

    def wait_wout():
        pltpu.make_async_copy(wout_hbm, wout, wout_sem).wait()

    middle = list(range(1, bottom))
    first, late = middle[0], middle[1:]
    rows = pl.ds(0, 3)
    pltpu.make_async_copy(lat_hbm.at[:, rows], lat.at[:, rows], lat_sem.at[0]).wait()
    for i in range(3):
        prepare(i)
    load_table.wait()
    load_index.wait()
    chosen = index_ref[...]
    decays = jnp.zeros(chosen.shape, jnp.float32)
    for level in range(table_ref.shape[0]):
        decays = jnp.where(chosen == level, table_ref[level], decays)
    growth = [decays]
    for _ in range(frames - 1):
        growth.append(growth[-1] * decays)
    load_win(0).wait()

    @block
    def _():
        partial[first] = times([wide[0]], win, [0])

    load_win(1).wait()
    load_win(2).wait()

    @block
    def _():
        value = times([wide[1]], win, [1]) + times([wide[2]], win, [2])
        states = scan(partial[first] + value)
        for frame in range(frames):
            partial[first, frame] = states[frame]

    rows = pl.ds(3, strip - 3)
    pltpu.make_async_copy(lat_hbm.at[:, rows], lat.at[:, rows], lat_sem.at[1]).wait()
    for i in range(3, strip):
        prepare(i)

    kept[...] = lat[:, 0]
    pl.semaphore_wait(barrier, total)

    leads = jnp.logical_and(jnp.logical_not(has_before), odd == 1)

    @pl.when(leads)
    def _():
        if positions > 1:
            begin(first)
        for i in late:
            drive(i)
            if positions > 1:
                begin(i)

    @block
    def _():
        offer(0)
        drive(0)

    send(0)

    @pl.when(jnp.logical_and(jnp.logical_not(has_before), odd == 0))
    def _():
        if positions > 1:
            begin(first)

    for tap in range(3):
        load_wout(tap).start()

    @pl.when(jnp.logical_not(leads))
    def _():
        for i in late:
            drive(i)
        offer(1)
        drive(bottom)

    @pl.when(leads)
    def _():
        offer(1)
        drive(bottom)

    send(1)

    def start():
        def far():
            absorb(0, 0)
            if positions > 1:
                begin(0)
            absorb(0, 1)
            if positions > 1:
                begin(ghost[0])

        def lead():
            if positions > 1:
                for i in late:
                    begin(i)

            @guard(1)
            def _():
                absorb(1, 0)

            if positions > 1:
                begin(bottom)

            def pass_turn():
                @guard(1)
                def _():
                    pl.semaphore_signal(turn, inc=1, device_id={"rows": near[1]}, device_id_type=MESH)

            @pl.when(has[0])
            def _():
                far()
                if positions > 1:
                    sent(1)
                    sent(0)
                    pass_turn()
                    sent(2)

            @pl.when(jnp.logical_not(has[0]))
            def _():
                if positions > 1:
                    begin(0)
                    sent(1)
                    pass_turn()
                    sent(0)

        def second():
            absorb(1, 0)
            if positions > 1:
                begin(bottom)
                pl.semaphore_wait(turn, 1)

            @pl.when(has[0])
            def _():
                far()

            if positions > 1:

                @pl.when(jnp.logical_not(has[0]))
                def _():
                    begin(0)

        @pl.when(odd == 0)
        def _():
            lead()

        @pl.when(odd == 1)
        def _():
            second()

        @guard(1)
        def _():
            absorb(1, 1)
            absorb_rest(1)

        wait_wout()

        @block
        def _():
            for i in range(1, strip):
                stretch(i, False)
            for i in range(2, bottom):
                write(i, product([i - 1, i, i + 1], i))
            if paired:
                stretch(ghost[1], False)
                write(bottom, product([bottom - 1, bottom], bottom) + reach(1))
            else:
                mixed[bottom] = product([bottom - 1, bottom], bottom)

        if not paired:

            @pl.when(has[1])
            def _():
                stretch(ghost[1], False)
                mixed[bottom] = mixed[bottom] + reach(1)

            write(bottom, mixed[bottom])

        @pl.when(has[0])
        def _():
            absorb_rest(0)

        @block
        def _():
            stretch(0, False)
            write(1, product([0, 1, 2], 1))
            mixed[0] = product([0, 1], 0)

        @pl.when(has[0])
        def _():
            stretch(ghost[0], False)
            mixed[0] = mixed[0] + reach(0)

        write(0, mixed[0])

    def follow(last):
        def receive(i, pieces=range(PIECES)):
            for piece in pieces:
                advance(i, piece, last)

        def receive_ghost():
            @pl.when(has[0])
            def _():
                absorb(0, 1)
                receive(ghost[0])

        def first_rows():
            stretch(first, True)
            for i in range(first + 2):
                mixed[i] = product([first], i)

        def late_rows():
            for i in late:
                stretch(i, True)
                mixed[i + 1] = product([i], i + 1)
                mixed[i - 1] = mixed[i - 1] + product([i], i - 1)
                mixed[i] = mixed[i] + product([i], i)

        def bottom_rows(done=False):
            stretch(bottom, True)
            mixed[bottom] = mixed[bottom] + product([bottom], bottom)
            mixed[bottom - 1] = mixed[bottom - 1] + product([bottom], bottom - 1)
            for i in range(2, bottom):
                write(i, mixed[i])
            if done:
                write(bottom, mixed[bottom])

        def far_rest():
            @pl.when(has[0])
            def _():
                absorb_rest(0)

        def top_rows():
            stretch(0, True)
            mixed[0] = mixed[0] + product([0], 0)
            write(1, mixed[1] + product([0], 1))

        def core_rows():
            @guard(1)
            def _():
                relay_copy().wait_recv()

                @block
                def _():
                    stretch(ghost[1], True)
                    mixed[bottom] = mixed[bottom] + reach(1)

        waits = jnp.logical_and(has[0], odd == 1)

        def core_close():
            if paired:
                relay_copy().wait_recv()
                stretch(ghost[1], True)
                write(bottom, mixed[bottom] + reach(1))
            else:
                core_rows()
                write(bottom, mixed[bottom])

        def ghost_rows():
            @pl.when(has[0])
            def _():
                stretch(ghost[0], True)
                write(0, mixed[0] + reach(0))

            @pl.when(jnp.logical_not(has[0]))
            def _():
                write(0, mixed[0])

        def early(act):
            (block if last else pl.when(odd == 1))(act)

        def later(act):
            if not last:
                pl.when(odd == 0)(act)

        wait_wout()
        receive(first)
        if last:
            block(first_rows)
        for i in late:
            receive(i)
        if not last:
            early(first_rows)
        early(late_rows)

        @guard(1)
        def _():
            absorb(1, 0)
            absorb(1, 1)
            absorb_rest(1)

        receive(bottom)

        @guard(1)
        def _():
            relay_copy().start()

        if last:

            block(bottom_rows)

            pl.when(jnp.logical_not(waits))(core_close)

        early_pieces, last_piece = range(PIECES - 1), [PIECES - 1]

        def top_half(half):
            part = pl.ds(half * cut, cut)
            stretch_half(0, half)
            one = mixed[1, :, part] + half_times(0, half, 0)
            two = mixed[0, :, part] + half_times(0, half, 1)
            write_half(1, half, one)
            write_half(0, half, two)

        def free_end():
            receive(0, early_pieces)
            top_half(0)
            receive(0, last_piece)
            top_half(1)

        def far_end():
            absorb(0, 0)
            receive(0)
            absorb_rest(0)
            block(top_rows)

            pl.when(odd == 1)(core_close)
            absorb(0, 1)
            receive(ghost[0])

            @block
            def _():
                stretch(ghost[0], True)
                write(0, mixed[0] + reach(0))

        if last:
            pl.when(jnp.logical_not(has[0]))(free_end)
            pl.when(has[0])(far_end)
        else:

            @pl.when(has[0])
            def _():
                absorb(0, 0)

            receive(0)
            receive_ghost()
            later(first_rows)
            later(late_rows)
            core_rows()
            block(lambda: bottom_rows(True))
            far_rest()
            block(top_rows)
            ghost_rows()

    @pl.when(jnp.logical_not(has_before))
    def _():
        start()

    @pl.when(jnp.logical_and(has_before, has_after))
    def _():
        follow(False)

    @pl.when(jnp.logical_and(has_before, jnp.logical_not(has_after)))
    def _():
        follow(True)

    for side in range(2):

        @pl.when(has[side])
        def _():
            share_sent(side)

    @pl.when(jnp.logical_and(has[1], has_before))
    def _():
        relay_copy().wait_send()

    pending = jnp.logical_and(has_after, jnp.logical_or(has_before, odd == 1))

    @pl.when(pending)
    def _():
        sent(1)
        sent(0)

    @pl.when(jnp.logical_and(has[0], pending))
    def _():
        sent(2)


def local(positions, strips, latents, weight_in, weight_out, decay_table, decay_index):
    frames, strip, width, channels = latents.shape
    link = jnp.bfloat16 if positions <= 8 else jnp.float32
    half = jnp.bfloat16
    dma = pltpu.SemaphoreType.DMA
    anywhere = pl.BlockSpec(memory_space=pl.ANY)
    done = pl.pallas_call(
        functools.partial(kernel, positions, strips),
        out_shape=[
            jax.ShapeDtypeStruct(latents.shape, latents.dtype),
            jax.ShapeDtypeStruct((frames, width, channels), latents.dtype),
            jax.ShapeDtypeStruct((frames, width, channels), jnp.float32),
        ],
        in_specs=[anywhere] * 5,
        out_specs=[pl.BlockSpec(memory_space=pltpu.VMEM)] * 3,
        scratch_shapes=[
            pltpu.VMEM((frames, strip, width, channels), half),
            pltpu.VMEM((9 * channels, channels), half),
            pltpu.VMEM((3, 3 * channels, channels), half),
            pltpu.VMEM((strip, frames, width, 3 * channels), half),
            pltpu.VMEM((strip + 2, frames, width, channels), jnp.float32),
            pltpu.VMEM((2, frames, 2, width, channels), half),
            pltpu.VMEM((2, frames, 2, width, channels), half),
            pltpu.VMEM((strip + 1, width, channels), link),
            pltpu.VMEM((strip + 1, width, channels), link),
            pltpu.VMEM((width, channels), link),
            pltpu.VMEM((strip, frames, width, channels), jnp.float32),
            pltpu.SMEM(decay_table.shape, jnp.float32),
            pltpu.VMEM((1, channels), jnp.int32),
            pltpu.VMEM((strip + 2, frames, width, 3 * channels), half),
            dma((2,)),
            dma((3,)),
            dma,
            dma((2,)),
            dma((2,)),
            dma((2, 3)),
            dma((3,)),
            dma((strip + 1, PIECES)),
            dma,
            dma,
            pltpu.SemaphoreType.REGULAR,
        ],
        compiler_params=pltpu.CompilerParams(collective_id=0, has_side_effects=True, vmem_limit_bytes=32 * 1024 * 1024),
    )(
        pltpu.with_memory_space_constraint(latents, pltpu.HBM),
        pltpu.with_memory_space_constraint(weight_in.reshape(3, 3 * channels, channels), pltpu.HBM),
        pltpu.with_memory_space_constraint(weight_out.reshape(3, 3 * channels, channels), pltpu.HBM),
        pltpu.with_memory_space_constraint(decay_table, pltpu.HBM),
        pltpu.with_memory_space_constraint(decay_index.reshape(1, channels), pltpu.HBM),
    )
    return pl.pallas_call(
        hand_out,
        out_shape=jax.ShapeDtypeStruct(latents.shape, latents.dtype),
        in_specs=[pl.BlockSpec(memory_space=pl.ANY)] + [pl.BlockSpec(memory_space=pltpu.VMEM)] * 2,
        out_specs=pl.BlockSpec(memory_space=pltpu.HBM),
        scratch_shapes=[pltpu.VMEM((frames, width, channels), half), dma((1 + frames,))],
    )(*[pltpu.with_memory_space_constraint(value, pltpu.VMEM) for value in done])


def hand_out(source, kept, open_row, target, row_out, sem):
    frames, strip = source.shape[:2]
    odd = lax.rem(lax.axis_index("rows"), 2)
    rest = pl.ds(1 - odd, strip - 1)
    first = pltpu.make_async_copy(source.at[:, rest], target.at[:, rest], sem.at[0])
    first.start()
    parts = []
    for frame in range(frames):
        row_out[frame] = update(kept[frame], open_row[frame])
        part = pltpu.make_async_copy(row_out.at[frame], target.at[frame, odd * (strip - 1)], sem.at[1 + frame])
        part.start()
        parts.append(part)
    first.wait()
    for part in parts:
        part.wait()


def solution(mesh):
    in_specs = (P(("groups", "tm"), "rows", None, None), P(), P(), P(), P())
    out_specs = P(("groups", "tm"), "rows", None, None)
    body = functools.partial(local, mesh.shape["tm"], mesh.shape["rows"])
    return jax.shard_map(body, mesh=mesh, in_specs=in_specs, out_specs=out_specs, check_vma=False)
```

```python
import functools
import math

import jax
import jax.numpy as jnp
from jax import lax
from jax.experimental import pallas as pl
from jax.experimental.pallas import tpu as pltpu
from jax.sharding import PartitionSpec as P

MESH = pl.DeviceIdType.MESH
PIECES = 4
ROOT = (2.0 / math.pi) ** 0.5
CUBIC = 0.044715 * ROOT


def update(base, x):
    half = 0.5 * x
    angle = x * (ROOT + CUBIC * (x * x))
    return (base.astype(jnp.float32) + (half + half * jnp.tanh(angle))).astype(jnp.bfloat16)


def kernel(
    positions,
    strips,
    lat_hbm,
    win_hbm,
    wout_hbm,
    table_hbm,
    index_hbm,
    out,
    kept,
    open_row,
    lat,
    win,
    wout,
    wide,
    partial,
    share,
    shared,
    carry,
    passed,
    relayed,
    mixed,
    table_ref,
    index_ref,
    wide_states,
    lat_sem,
    win_sem,
    small_sem,
    share_send,
    share_recv,
    carry_send,
    carry_recv,
    relay_send,
    relay_recv,
    turn,
):
    frames, strip, width, channels = lat.shape
    row = lax.axis_index("rows")
    moment = lax.axis_index("tm")
    odd = lax.rem(row, 2)
    span = width // PIECES
    bottom = strip - 1
    final = frames - 1
    edge = (0, bottom)
    ghost = (strip, strip + 1)
    near = (row - 1 + 2 * odd, row + 1 - 2 * odd)
    has = tuple(jnp.logical_and(at >= 0, at < strips) for at in near)
    paired = strips % 2 == 0
    depth = 3 * channels
    has_before, has_after = moment > 0, moment < positions - 1

    def guard(side):
        if side == 1 and paired:
            return lambda act: act()
        return pl.when(has[side])

    def place(i, count):
        return i + odd * (count - 1 - 2 * i)

    def load_lat(i):
        return pltpu.make_async_copy(lat_hbm.at[:, place(i, strip)], lat.at[:, i], lat_sem.at[0 if i < 3 else 1])

    def load_win(tap):
        return pltpu.make_async_copy(win_hbm.at[place(tap, 3)], win.at[pl.ds(tap * depth, depth)], win_sem.at[tap])

    def load_wout(tap):
        return pltpu.make_async_copy(wout_hbm.at[place(tap, 3)], wout.at[tap], win_sem.at[0])

    load_table = pltpu.make_async_copy(table_hbm, table_ref, small_sem.at[0])
    load_index = pltpu.make_async_copy(index_hbm, index_ref, small_sem.at[1])

    for i in range(3):
        load_lat(i).start()
    load_win(0).start()

    barrier = pltpu.get_barrier_semaphore()
    greeted = (
        (has[0], {"rows": near[0]}),
        (has[1], {"rows": near[1]}),
        (has_before, {"tm": moment - 1}),
        (has_after, {"tm": moment + 1}),
    )
    total = 0
    for exists, where in greeted:
        total = total + exists.astype(jnp.int32)

        @pl.when(exists)
        def _():
            pl.semaphore_signal(barrier, inc=1, device_id=where, device_id_type=MESH)

    load_table.start()
    load_index.start()
    for tap in range(1, 3):
        load_win(tap).start()
    for i in range(3, strip):
        load_lat(i).start()

    def share_copy(side, kind, frame):
        return pltpu.make_async_remote_copy(
            src_ref=share.at[side, frame, kind],
            dst_ref=shared.at[side, frame, kind],
            send_sem=share_send.at[side],
            recv_sem=share_recv.at[side, kind if frame == final else 2],
            device_id={"rows": near[side]},
            device_id_type=MESH,
        )

    def relay_copy():
        return pltpu.make_async_remote_copy(
            src_ref=carry.at[bottom],
            dst_ref=relayed,
            send_sem=relay_send,
            recv_sem=relay_recv,
            device_id={"rows": near[1]},
            device_id_type=MESH,
        )

    def carry_copy(i, piece):
        part = pl.ds(piece * span, span)
        return pltpu.make_async_remote_copy(
            src_ref=passed.at[i, part],
            dst_ref=carry.at[i, part],
            send_sem=carry_send.at[min(i, 1) if i < strip else 2],
            recv_sem=carry_recv.at[i, piece],
            device_id={"tm": moment + 1},
            device_id_type=MESH,
        )

    column = lax.broadcasted_iota(jnp.int32, (width, channels), 0)

    def spread(value):
        full = value.astype(jnp.float32)
        before = jnp.where(column == 0, 0.0, pltpu.roll(full, 1, 0))
        after = jnp.where(column == width - 1, 0.0, pltpu.roll(full, width - 1, 0))
        middle = value.astype(jnp.bfloat16)
        return jnp.concatenate([before.astype(jnp.bfloat16), middle, after.astype(jnp.bfloat16)], axis=-1)

    def prepare(i):
        for frame in range(frames):
            wide[i, frame] = spread(lat[frame, i])

    def times(rows, weights, taps):
        window = [r.reshape(frames * width, 3 * channels) for r in rows]
        window = window[0] if len(rows) == 1 else jnp.concatenate(window, axis=-1)
        if len(weights.shape) == 3:
            factor = weights[taps[0] : taps[-1] + 1].reshape(len(taps) * depth, channels)
        else:
            factor = weights[taps[0] * depth : (taps[-1] + 1) * depth]
        value = jnp.dot(window, factor, preferred_element_type=jnp.float32)
        return value.reshape(frames, width, channels)

    def scan(value):
        running = [value[0]]
        for frame in range(1, frames):
            running.append(decays * running[-1] + value[frame])
        return running

    def drive(i):
        taps = [tap for tap in range(3) if 0 <= i + tap - 1 < strip]
        states = scan(times([wide[i + tap - 1] for tap in taps], win, taps))
        for frame in range(frames):
            partial[i, frame] = states[frame]
            if i in edge:
                share[edge.index(i), frame, 1] = states[frame].astype(jnp.bfloat16)

    def offer(side):
        states = scan(times([wide[edge[side]]], win, [2 - 2 * side]))
        for frame in range(frames):
            partial[ghost[side], frame] = states[frame]
            share[side, frame, 0] = states[frame].astype(jnp.bfloat16)

    def send(side):
        @guard(side)
        def _():
            for frame in reversed(range(frames)):
                for kind in range(2):
                    share_copy(side, kind, frame).start()

    def add_share(side, kind, frame):
        i = (edge, ghost)[kind][side]
        partial[i, frame] = partial[i, frame] + shared[side, frame, kind].astype(jnp.float32)

    def absorb(side, kind):
        share_copy(side, kind, final).wait_recv()
        add_share(side, kind, final)

    def absorb_rest(side):
        if final == 0:
            return
        part = pl.ds(0, final)
        pltpu.make_async_remote_copy(
            src_ref=share.at[side, part],
            dst_ref=shared.at[side, part],
            send_sem=share_send.at[side],
            recv_sem=share_recv.at[side, 2],
            device_id={"rows": near[side]},
            device_id_type=MESH,
        ).wait_recv()
        for frame in range(final):
            for kind in range(2):
                add_share(side, kind, frame)

    def share_sent(side):
        pltpu.make_async_remote_copy(
            src_ref=share.at[side],
            dst_ref=shared.at[side],
            send_sem=share_send.at[side],
            recv_sem=share_recv.at[side, 2],
            device_id={"rows": near[side]},
            device_id_type=MESH,
        ).wait_send()

    def block(act):
        pl.when(row >= 0)(act)

    def begin(i, pieces=range(PIECES)):
        for piece in pieces:
            part = pl.ds(piece * span, span)
            passed[i, part] = partial[i, final, part].astype(passed.dtype)
            carry_copy(i, piece).start()

    def advance(i, piece, last):
        part = pl.ds(piece * span, span)
        carry_copy(i, piece).wait_recv()
        if not last:
            value = partial[i, final, part] + growth[final] * carry[i, part].astype(jnp.float32)
            passed[i, part] = value.astype(passed.dtype)
            carry_copy(i, piece).start()

    def sent(group):
        part = (pl.ds(0, 1), pl.ds(1, strip - 1), pl.ds(strip, 1))[group]
        pltpu.make_async_remote_copy(
            src_ref=passed.at[part],
            dst_ref=carry.at[part],
            send_sem=carry_send.at[(0, 1, 2)[group]],
            recv_sem=carry_recv.at[0, 0],
            device_id={"tm": moment + 1},
            device_id_type=MESH,
        ).wait_send()

    def stretch(i, carried):
        if carried:
            arrived = (relayed[...] if i == ghost[1] else carry[i]).astype(jnp.float32)
        for frame in range(frames):
            state = partial[i, frame]
            if carried:
                state = state + growth[frame] * arrived
            wide_states[i, frame] = spread(state)

    def product(sources, i):
        taps = [source - i + 1 for source in sources]
        return times([wide_states[source] for source in sources], wout, taps)

    def write(i, value):
        for frame in range(frames):
            if i == 0:
                open_row[frame] = value[frame]
                continue
            out[frame, place(i, strip)] = update(lat[frame, i], value[frame])

    cut = width // 2

    def stretch_half(i, half):
        low, count = (0, cut + span) if half == 0 else (cut - span, cut + span)
        part = pl.ds(low, count)
        keep = slice(0, cut) if half == 0 else slice(span, span + cut)
        place_of = lax.broadcasted_iota(jnp.int32, (count, channels), 0)
        arrived = carry[i, part].astype(jnp.float32)
        for frame in range(frames):
            full = partial[i, frame, part] + growth[frame] * arrived
            before, after = pltpu.roll(full, 1, 0), pltpu.roll(full, count - 1, 0)
            if half == 0:
                before = jnp.where(place_of == 0, 0.0, before)
            else:
                after = jnp.where(place_of == count - 1, 0.0, after)
            whole = jnp.concatenate([v.astype(jnp.bfloat16) for v in (before, full, after)], axis=-1)
            wide_states[i, frame, pl.ds(half * cut, cut)] = whole[keep]

    def half_times(i, half, tap):
        window = wide_states[i, :, pl.ds(half * cut, cut)].reshape(frames * cut, 3 * channels)
        value = jnp.dot(window, wout[tap], preferred_element_type=jnp.float32)
        return value.reshape(frames, cut, channels)

    def write_half(i, half, value):
        part = pl.ds(half * cut, cut)
        for frame in range(frames):
            if i == 0:
                open_row[frame, part] = value[frame]
                continue
            out[frame, place(i, strip), part] = update(lat[frame, i, part], value[frame])

    def reach(side):
        return times([wide_states[ghost[side]]], wout, [2 * side])

    def wait_wout():
        pltpu.make_async_copy(wout_hbm, wout, win_sem.at[0]).wait()

    middle = list(range(1, bottom))
    first, late = middle[0], middle[1:]
    rows = pl.ds(0, 3)
    pltpu.make_async_copy(lat_hbm.at[:, rows], lat.at[:, rows], lat_sem.at[0]).wait()
    for i in range(3):
        prepare(i)
    load_table.wait()
    load_index.wait()
    chosen = index_ref[...]
    decays = jnp.zeros(chosen.shape, jnp.float32)
    for level in range(table_ref.shape[0]):
        decays = jnp.where(chosen == level, table_ref[level], decays)
    growth = [decays]
    for _ in range(frames - 1):
        growth.append(growth[-1] * decays)
    load_win(0).wait()

    @block
    def _():
        partial[first] = times([wide[0]], win, [0])

    load_win(1).wait()
    load_win(2).wait()

    @block
    def _():
        value = times([wide[1]], win, [1]) + times([wide[2]], win, [2])
        states = scan(partial[first] + value)
        for frame in range(frames):
            partial[first, frame] = states[frame]

    rows = pl.ds(3, strip - 3)
    pltpu.make_async_copy(lat_hbm.at[:, rows], lat.at[:, rows], lat_sem.at[1]).wait()
    for i in range(3, strip):
        prepare(i)

    kept[...] = lat[:, 0]
    pl.semaphore_wait(barrier, total)

    leads = jnp.logical_and(jnp.logical_not(has_before), odd == 1)

    @pl.when(leads)
    def _():
        if positions > 1:
            begin(first)
        for i in late:
            drive(i)
            if positions > 1:
                begin(i)

    @block
    def _():
        offer(0)
        drive(0)

    send(0)

    @pl.when(jnp.logical_and(jnp.logical_not(has_before), odd == 0))
    def _():
        if positions > 1:
            begin(first)

    for tap in range(3):
        load_wout(tap).start()

    @pl.when(jnp.logical_not(leads))
    def _():
        for i in late:
            drive(i)
        offer(1)
        drive(bottom)

    @pl.when(leads)
    def _():
        offer(1)
        drive(bottom)

    send(1)

    def start():
        def far():
            absorb(0, 0)
            if positions > 1:
                begin(0)
            absorb(0, 1)
            if positions > 1:
                begin(ghost[0])

        def lead():
            if positions > 1:
                for i in late:
                    begin(i)

            @guard(1)
            def _():
                absorb(1, 0)

            if positions > 1:
                begin(bottom)

            def pass_turn():
                @guard(1)
                def _():
                    pl.semaphore_signal(turn, inc=1, device_id={"rows": near[1]}, device_id_type=MESH)

            @pl.when(has[0])
            def _():
                far()
                if positions > 1:
                    sent(1)
                    sent(0)
                    pass_turn()
                    sent(2)

            @pl.when(jnp.logical_not(has[0]))
            def _():
                if positions > 1:
                    begin(0)
                    sent(1)
                    pass_turn()
                    sent(0)

        def second():
            absorb(1, 0)
            if positions > 1:
                begin(bottom)
                pl.semaphore_wait(turn, 1)

            @pl.when(has[0])
            def _():
                far()

            if positions > 1:

                @pl.when(jnp.logical_not(has[0]))
                def _():
                    begin(0)

        @pl.when(odd == 0)
        def _():
            lead()

        @pl.when(odd == 1)
        def _():
            second()

        @guard(1)
        def _():
            absorb(1, 1)
            absorb_rest(1)

        wait_wout()

        @block
        def _():
            for i in range(1, strip):
                stretch(i, False)
            for i in range(2, bottom):
                write(i, product([i - 1, i, i + 1], i))
            if paired:
                stretch(ghost[1], False)
                write(bottom, product([bottom - 1, bottom], bottom) + reach(1))
            else:
                mixed[bottom] = product([bottom - 1, bottom], bottom)

        if not paired:

            @pl.when(has[1])
            def _():
                stretch(ghost[1], False)
                mixed[bottom] = mixed[bottom] + reach(1)

            write(bottom, mixed[bottom])

        @pl.when(has[0])
        def _():
            absorb_rest(0)

        @block
        def _():
            stretch(0, False)
            write(1, product([0, 1, 2], 1))
            mixed[0] = product([0, 1], 0)

        @pl.when(has[0])
        def _():
            stretch(ghost[0], False)
            mixed[0] = mixed[0] + reach(0)

        write(0, mixed[0])

    def follow(last):
        def receive(i, pieces=range(PIECES)):
            for piece in pieces:
                advance(i, piece, last)

        def receive_ghost():
            @pl.when(has[0])
            def _():
                absorb(0, 1)
                receive(ghost[0])

        def first_rows():
            stretch(first, True)
            for i in range(first + 2):
                mixed[i] = product([first], i)

        def late_rows():
            for i in late:
                stretch(i, True)
                mixed[i + 1] = product([i], i + 1)
                mixed[i - 1] = mixed[i - 1] + product([i], i - 1)
                mixed[i] = mixed[i] + product([i], i)

        def bottom_rows(done=False):
            stretch(bottom, True)
            mixed[bottom] = mixed[bottom] + product([bottom], bottom)
            mixed[bottom - 1] = mixed[bottom - 1] + product([bottom], bottom - 1)
            for i in range(2, bottom):
                write(i, mixed[i])
            if done:
                write(bottom, mixed[bottom])

        def far_rest():
            @pl.when(has[0])
            def _():
                absorb_rest(0)

        def top_rows():
            stretch(0, True)
            mixed[0] = mixed[0] + product([0], 0)
            write(1, mixed[1] + product([0], 1))

        def core_rows():
            @guard(1)
            def _():
                relay_copy().wait_recv()

                @block
                def _():
                    stretch(ghost[1], True)
                    mixed[bottom] = mixed[bottom] + reach(1)

        waits = jnp.logical_and(has[0], odd == 1)

        def core_close():
            if paired:
                relay_copy().wait_recv()
                stretch(ghost[1], True)
                write(bottom, mixed[bottom] + reach(1))
            else:
                core_rows()
                write(bottom, mixed[bottom])

        def ghost_rows():
            @pl.when(has[0])
            def _():
                stretch(ghost[0], True)
                write(0, mixed[0] + reach(0))

            @pl.when(jnp.logical_not(has[0]))
            def _():
                write(0, mixed[0])

        def early(act):
            (block if last else pl.when(odd == 1))(act)

        def later(act):
            if not last:
                pl.when(odd == 0)(act)

        wait_wout()
        receive(first)
        if last:
            block(first_rows)
        for i in late:
            receive(i)
        if not last:
            early(first_rows)
        early(late_rows)

        @guard(1)
        def _():
            absorb(1, 0)
            absorb(1, 1)
            absorb_rest(1)

        receive(bottom)

        @guard(1)
        def _():
            relay_copy().start()

        if last:

            block(bottom_rows)

            pl.when(jnp.logical_not(waits))(core_close)

        early_pieces, last_piece = range(PIECES - 1), [PIECES - 1]

        def top_half(half):
            part = pl.ds(half * cut, cut)
            stretch_half(0, half)
            one = mixed[1, :, part] + half_times(0, half, 0)
            two = mixed[0, :, part] + half_times(0, half, 1)
            write_half(1, half, one)
            write_half(0, half, two)

        def free_end():
            receive(0, early_pieces)
            top_half(0)
            receive(0, last_piece)
            top_half(1)

        def far_end():
            absorb(0, 0)
            receive(0)
            absorb_rest(0)
            block(top_rows)

            pl.when(odd == 1)(core_close)
            absorb(0, 1)
            receive(ghost[0])

            @block
            def _():
                stretch(ghost[0], True)
                write(0, mixed[0] + reach(0))

        if last:
            pl.when(jnp.logical_not(has[0]))(free_end)
            pl.when(has[0])(far_end)
        else:

            @pl.when(has[0])
            def _():
                absorb(0, 0)

            receive(0)
            receive_ghost()
            later(first_rows)
            later(late_rows)
            core_rows()
            block(lambda: bottom_rows(True))
            far_rest()
            block(top_rows)
            ghost_rows()

    @pl.when(jnp.logical_not(has_before))
    def _():
        start()

    @pl.when(jnp.logical_and(has_before, has_after))
    def _():
        follow(False)

    @pl.when(jnp.logical_and(has_before, jnp.logical_not(has_after)))
    def _():
        follow(True)

    for side in range(2):

        @pl.when(has[side])
        def _():
            share_sent(side)

    @pl.when(jnp.logical_and(has[1], has_before))
    def _():
        relay_copy().wait_send()

    pending = jnp.logical_and(has_after, jnp.logical_or(has_before, odd == 1))

    @pl.when(pending)
    def _():
        sent(1)
        sent(0)

    @pl.when(jnp.logical_and(has[0], pending))
    def _():
        sent(2)


def local(positions, strips, latents, weight_in, weight_out, decay_table, decay_index):
    frames, strip, width, channels = latents.shape
    link = jnp.bfloat16 if positions <= 8 else jnp.float32
    half = jnp.bfloat16
    dma = pltpu.SemaphoreType.DMA
    anywhere = pl.BlockSpec(memory_space=pl.ANY)
    done = pl.pallas_call(
        functools.partial(kernel, positions, strips),
        out_shape=[
            jax.ShapeDtypeStruct(latents.shape, latents.dtype),
            jax.ShapeDtypeStruct((frames, width, channels), latents.dtype),
            jax.ShapeDtypeStruct((frames, width, channels), jnp.float32),
        ],
        in_specs=[anywhere] * 5,
        out_specs=[pl.BlockSpec(memory_space=pltpu.VMEM)] * 3,
        scratch_shapes=[
            pltpu.VMEM((frames, strip, width, channels), half),
            pltpu.VMEM((9 * channels, channels), half),
            pltpu.VMEM((3, 3 * channels, channels), half),
            pltpu.VMEM((strip, frames, width, 3 * channels), half),
            pltpu.VMEM((strip + 2, frames, width, channels), jnp.float32),
            pltpu.VMEM((2, frames, 2, width, channels), half),
            pltpu.VMEM((2, frames, 2, width, channels), half),
            pltpu.VMEM((strip + 1, width, channels), link),
            pltpu.VMEM((strip + 1, width, channels), link),
            pltpu.VMEM((width, channels), link),
            pltpu.VMEM((strip, frames, width, channels), jnp.float32),
            pltpu.SMEM(decay_table.shape, jnp.float32),
            pltpu.VMEM((1, channels), jnp.int32),
            pltpu.VMEM((strip + 2, frames, width, 3 * channels), half),
            dma((2,)),
            dma((3,)),
            dma((2,)),
            dma((2,)),
            dma((2, 3)),
            dma((3,)),
            dma((strip + 1, PIECES)),
            dma,
            dma,
            pltpu.SemaphoreType.REGULAR,
        ],
        compiler_params=pltpu.CompilerParams(collective_id=0, has_side_effects=True, vmem_limit_bytes=32 * 1024 * 1024),
    )(
        pltpu.with_memory_space_constraint(latents, pltpu.HBM),
        pltpu.with_memory_space_constraint(weight_in.reshape(3, 3 * channels, channels), pltpu.HBM),
        pltpu.with_memory_space_constraint(weight_out.reshape(3, 3 * channels, channels), pltpu.HBM),
        pltpu.with_memory_space_constraint(decay_table, pltpu.HBM),
        pltpu.with_memory_space_constraint(decay_index.reshape(1, channels), pltpu.HBM),
    )
    return pl.pallas_call(
        hand_out,
        out_shape=jax.ShapeDtypeStruct(latents.shape, latents.dtype),
        in_specs=[pl.BlockSpec(memory_space=pl.ANY)] + [pl.BlockSpec(memory_space=pltpu.VMEM)] * 2,
        out_specs=pl.BlockSpec(memory_space=pltpu.HBM),
        scratch_shapes=[pltpu.VMEM((frames, width, channels), half), dma((1 + frames,))],
    )(*[pltpu.with_memory_space_constraint(value, pltpu.VMEM) for value in done])


def hand_out(source, kept, open_row, target, row_out, sem):
    frames, strip = source.shape[:2]
    odd = lax.rem(lax.axis_index("rows"), 2)
    rest = pl.ds(1 - odd, strip - 1)
    first = pltpu.make_async_copy(source.at[:, rest], target.at[:, rest], sem.at[0])
    first.start()
    parts = []
    for frame in range(frames):
        row_out[frame] = update(kept[frame], open_row[frame])
        part = pltpu.make_async_copy(row_out.at[frame], target.at[frame, odd * (strip - 1)], sem.at[1 + frame])
        part.start()
        parts.append(part)
    first.wait()
    for part in parts:
        part.wait()


def solution(mesh):
    in_specs = (P(("groups", "tm"), "rows", None, None), P(), P(), P(), P())
    out_specs = P(("groups", "tm"), "rows", None, None)
    body = functools.partial(local, mesh.shape["tm"], mesh.shape["rows"])
    return jax.shard_map(body, mesh=mesh, in_specs=in_specs, out_specs=out_specs, check_vma=False)
```
